256 devices in a mesh: dp: 256 (over y, z, x, core).
Axes of the slice: x: 4, y: 4, z: 8, core: 2. Of those that a mesh axis runs over, the one named last changes fastest.
Arguments:
- tokens: float32 [65536, 1024], P('dp'), may hold values from -24 to 24
- cotangent: float32 [65536, 1024], P('dp'), may hold values from -6 to 6
- weight: float32 [1024, 1024], replicated, may hold values from -0.1875 to 0.1875
- first_moment: float32 [1024, 1024], P('dp'), may hold values from -0.6 to 0.6
- second_moment: float32 [1024, 1024], P('dp'), may hold values from 0.001 to 0.1
Outputs:
- projected: float32 [65536, 1024], P('dp')
- input_grad: float32 [65536, 1024], P('dp')
- new_weight: float32 [1024, 1024], replicated
- new_first: float32 [1024, 1024], P('dp')
- new_second: float32 [1024, 1024], P('dp')
- next_projected: float32 [65536, 1024], P('dp')
The draws below stay inside these ranges and needn't reach their ends.
All inputs are finite; a program needn't handle non-finite values.
Results may differ from the reference program's by a relative error of at most 0.00017.
Values sent between devices are 32-bit elements; how exact they have to be, the bound alone decides.
A program may use at most 64 MiB of HBM per device.

```python
import math
import jax
import jax.numpy as jnp
from jax import lax

D = 1024
TOK_DEV = 256
TOKENS = 65536
N_DP = 256


def raised(result, own_key, source, target, blocks, factor):
    def block_of(dim):
        return (jnp.arange(result.shape[dim]) // (result.shape[dim] // blocks)).reshape((-1,) + (1,) * (result.ndim - 1 - dim))

    one_side = jax.random.permutation(own_key, blocks)[block_of(target)]
    far = (block_of(target) + blocks // 2) % blocks
    return jnp.where((block_of(source) == one_side) | (block_of(source) == far), factor * result, result)


def block_scale(key, dims, split, smallest, high):
    gain, own = 1.0, jax.random.fold_in(key, 6)
    for axis_at, parts in split:
        draws = jnp.exp(jax.random.uniform(jax.random.fold_in(own, axis_at), (parts,), jnp.float32, smallest / len(split), high / len(split)))
        gain = gain * jnp.repeat(draws, dims[axis_at] // parts).reshape([-1 if axis == axis_at else 1 for axis in range(len(dims))])
    return gain


def bell_draw(rng, shape, spread, reach, split=(), held_as=jnp.bfloat16):
    values = jax.random.normal(rng, shape, jnp.float32) * spread
    if len(split) > 0:
        values = block_scale(rng, shape, split, -0.22, 0.18) * values
    return jnp.clip(values, min=-reach, max=reach).astype(held_as)


def noise_with(own_key, extent, deviation, limit, shards, heavy, held_as=jnp.bfloat16):
    values = deviation * jax.random.normal(own_key, extent, jnp.float32)
    if shards:
        values = values * block_scale(own_key, extent, shards, -0.22, 0.18)
    return jnp.clip(raised(values, jax.random.fold_in(own_key, 3), *heavy), -limit, limit).astype(held_as)


def setup_inputs(seed: int = 0) -> dict:
    streams_of = jax.random.split(jax.random.key(seed), 6)
    tokens = noise_with(streams_of[0], (TOKENS, D), 1.0, 24.0, ((0, 256),), (0, 1, 256, 6.0), jnp.float32)
    cotangent = bell_draw(streams_of[1], (TOKENS, D), 1.0, 6.0, ((0, 256),), jnp.float32)
    weight = bell_draw(streams_of[2], (D, D), D ** -0.5, 0.1875, (), jnp.float32)
    first_moment = bell_draw(streams_of[3], (D, D), 0.1, 0.6, ((0, 256),), jnp.float32)
    second_moment = jnp.clip(jnp.exp(math.log(0.1) - 4.6051702 * jax.random.uniform(streams_of[4], (D, D), jnp.float32) ** block_scale(streams_of[4], (D, D), ((0, 256),), -0.2, 0.2)), 0.001, 0.1)
    return dict(tokens=tokens, cotangent=cotangent, weight=weight, first_moment=first_moment, second_moment=second_moment)


beta_one = 0.9
beta_two = 0.999
rate_value = 0.01
step_count = 10
adam_epsilon = 1e-08
norm_epsilon = 1e-06

def combine(left_rows, right_rows):
    cross_term = lax.optimization_barrier(jnp.sum(left_rows * right_rows, axis=-1, keepdims=True))
    left_norm = lax.optimization_barrier(jnp.sum(left_rows * left_rows, axis=-1, keepdims=True))
    right_norm = lax.optimization_barrier(jnp.sum(right_rows * right_rows, axis=-1, keepdims=True))
    left_coef = 1.0 - cross_term / (2.0 * (left_norm + norm_epsilon))
    right_coef = 1.0 - cross_term / (2.0 * (right_norm + norm_epsilon))
    return left_coef * left_rows + right_coef * right_rows

def adam_update(gradient, weight_rows, first_rows, second_rows):
    first_new = beta_one * first_rows + (1.0 - beta_one) * gradient
    second_new = beta_two * second_rows + (1.0 - beta_two) * gradient * gradient
    first_hat = first_new / (1.0 - beta_one ** step_count)
    second_hat = second_new / (1.0 - beta_two ** step_count)
    weight_new = weight_rows - rate_value * first_hat / (jnp.sqrt(second_hat) + adam_epsilon)
    return (weight_new, first_new, second_new)

def reference(tokens, cotangent, weight, first_moment, second_moment):
    highest = lax.Precision.HIGHEST
    projected = jnp.dot(tokens, weight, precision=highest, preferred_element_type=jnp.float32)
    input_grad = lax.dot_general(cotangent, weight, (((1,), (1,)), ((), ())), precision=highest, preferred_element_type=jnp.float32)
    token_groups = tokens.reshape(N_DP, TOK_DEV, D)
    cotangent_groups = cotangent.reshape(N_DP, TOK_DEV, D)
    stride = 64 if D % 64 == 0 else D
    block_count = D // stride

    def block_rows(start):
        columns = lax.dynamic_slice_in_dim(token_groups, start, stride, 2)
        stacked = jnp.einsum('ntr,ntc->nrc', columns, cotangent_groups, precision=highest) / TOK_DEV
        while stacked.shape[0] > 1:
            halfway = stacked.shape[0] // 2
            stacked = combine(stacked[:halfway], stacked[halfway:])
        return stacked[0]
    starts = (jnp.arange(block_count) * stride).astype(jnp.int32)
    summed_grad = lax.map(block_rows, starts).reshape(D, D)
    new_weight, new_first, new_second = adam_update(summed_grad, weight, first_moment, second_moment)
    next_projected = jnp.dot(tokens, new_weight, precision=highest, preferred_element_type=jnp.float32)
    return (projected, input_grad, new_weight, new_first, new_second, next_projected)
```

```python
import jax
import jax.numpy as jnp
from jax import lax
from jax.experimental import pallas as pl
from jax.experimental.pallas import tpu as pltpu
from jax.sharding import PartitionSpec as P

beta_one = 0.9
beta_two = 0.999
rate_value = 0.01
step_count = 10
adam_epsilon = 1e-08
norm_epsilon = 1e-06

MESH = pl.DeviceIdType.MESH
NY, NZ, NX = 4, 8, 4
D = 1024
T = 256
CH = D // (NY * NZ)
F32, BF16 = jnp.float32, jnp.bfloat16


def combine(left_rows, right_rows):
    cross_term = jnp.sum(left_rows * right_rows, axis=-1, keepdims=True)
    left_norm = jnp.sum(left_rows * left_rows, axis=-1, keepdims=True)
    right_norm = jnp.sum(right_rows * right_rows, axis=-1, keepdims=True)
    left_coef = 1.0 - cross_term / (2.0 * (left_norm + norm_epsilon))
    right_coef = 1.0 - cross_term / (2.0 * (right_norm + norm_epsilon))
    return left_coef * left_rows + right_coef * right_rows


def adam_update(gradient, weight_rows, first_rows, second_rows):
    first_new = beta_one * first_rows + (1.0 - beta_one) * gradient
    second_new = beta_two * second_rows + (1.0 - beta_two) * gradient * gradient
    first_hat = first_new / (1.0 - beta_one**step_count)
    second_hat = second_new / (1.0 - beta_two**step_count)
    weight_new = weight_rows - rate_value * first_hat / (jnp.sqrt(second_hat) + adam_epsilon)
    return (weight_new, first_new, second_new)


def split(value):
    high = value.astype(BF16)
    return high, (value - high.astype(F32)).astype(BF16)


def dot(a, b, contract):
    return lax.dot_general(a, b, (contract, ((), ())), preferred_element_type=F32)


def dot3(a_high, a_low, b_high, b_low, contract):
    return (
        dot(a_high, b_high, contract)
        + dot(a_high, b_low, contract)
        + dot(a_low, b_high, contract)
    )


def offset_of(s):
    return 4 + (s + 1) // 2 * (1 - 2 * (s % 2))


def exchange_kernel(
    tok_hbm, cot_hbm, w_hbm, m_hbm, v_hbm,
    proj_o, igrad_o, w_o, m_o, v_o,
    tok_v, cot_v, w_v, tth, ttl, th, tl, ch, cl,
    g, yr, zs, zr, xs, xr, cs, cr, own_mv, sib_mv, new_mv, wbuf, proj_v, igrad_v,
    in_sem, out_sem, ys_sem, yr_sem, zs_sem, zr_sem, xs_sem, xr_sem, cs_sem, cr_sem,
    gzs_sem, gzr_sem, gxs_sem, gxr_sem, gys_sem, gyr_sem,
    gas_sem, gar_sem, gbs_sem, gbr_sem, gss_sem, gsr_sem, wo_sem,
):
    me = lax.axis_index("dp")
    c = me % 2
    x = me // 2 % NX
    z = me // (2 * NX) % NZ
    y = me // (2 * NX * NZ)

    def device(yy, zz, xx, cc):
        return (((yy * NZ + zz) * NX + xx) * 2 + cc,)

    def at_y(d):
        return device((y + d) % NY, z, x, c)

    def at_z(d):
        return device(y, (z + d) % NZ, x, c)

    def at_x(d):
        return device(y, z, (x + d) % NX, c)

    sibling = device(y, z, x, 1 - c)

    def remote(src, dst, send, recv, target):
        return pltpu.make_async_remote_copy(
            src_ref=src, dst_ref=dst, send_sem=send, recv_sem=recv,
            device_id=target, device_id_type=MESH,
        )

    loads = [
        pltpu.make_async_copy(src, dst, in_sem.at[i])
        for i, (src, dst) in enumerate(
            [
                (tok_hbm, tok_v),
                (cot_hbm, cot_v),
                (m_hbm, own_mv.at[0]),
                (v_hbm, own_mv.at[1]),
                (w_hbm, w_v),
            ]
        )
    ]
    for load in loads:
        load.start()

    barrier = pltpu.get_barrier_semaphore()
    partners = (
        [at_y(d) for d in range(1, NY)]
        + [at_z(d) for d in range(1, NZ)]
        + [at_x(d) for d in range(1, NX)]
        + [sibling]
    )
    for partner in partners:
        pl.semaphore_signal(barrier, inc=1, device_id=partner, device_id_type=MESH)

    loads[0].wait()
    for j in range(D // 128):
        lanes = slice(128 * j, 128 * j + 128)
        piece = tok_v[:, lanes]
        th[:, lanes], tl[:, lanes] = split(piece)
        tth[lanes, :], ttl[lanes, :] = split(piece.T * (1.0 / T))
    loads[1].wait()
    for j in range(D // 256):
        lanes = slice(256 * j, 256 * j + 256)
        ch[:, lanes], cl[:, lanes] = split(cot_v[:, lanes])
    loads[2].wait()
    loads[3].wait()
    pl.semaphore_wait(barrier, len(partners))

    mv_copy = remote(own_mv, sib_mv, cs_sem.at[1], cr_sem.at[1], sibling)
    mv_copy.start()

    def y_copy(s, d):
        return remote(g.at[s, d], yr.at[d - 1, s], ys_sem.at[d - 1, s], yr_sem.at[d - 1, s], at_y(d))

    def z_copy(s, d):
        return remote(zs.at[s], zr.at[d - 1], zs_sem.at[d - 1], zr_sem.at[d - 1], at_z(d))

    def gradient_step(s, carry):
        owner = (z + offset_of(s)) % NZ
        starts = [
            pl.multiple_of((y + d) % NY * (D // NY) + owner * CH, CH) for d in range(NY)
        ]
        high = [tth[pl.ds(start, CH), :] for start in starts]
        low = [ttl[pl.ds(start, CH), :] for start in starts]
        count = NY * CH
        both = dot(jnp.concatenate(high + low, axis=0), ch[...], ((1,), (0,)))
        rest = dot(jnp.concatenate(high, axis=0), cl[...], ((1,), (0,)))
        value = both[:count] + both[count:] + rest
        for d in range(NY):
            g[s, d] = value[d * CH : (d + 1) * CH]
        for d in range(1, NY):
            y_copy(s, d).start()
        return carry

    lax.fori_loop(0, NZ, gradient_step, 0)

    loads[4].wait()

    def y_combined(s):
        for d in range(1, NY):
            y_copy(s, d).wait_recv()
        return combine(combine(g[s, 0], yr[1, s]), combine(yr[0, s], yr[2, s]))

    def filler(s):
        @pl.when(s < 4)
        def _():
            lanes = pl.ds(pl.multiple_of(s * 256, 256), 256)
            wh, wl = split(w_v[:, lanes])
            proj_v[:, lanes] = dot3(th[...], tl[...], wh, wl, ((1,), (0,)))

        @pl.when(s >= 4)
        def _():
            lanes = pl.ds(pl.multiple_of((s - 4) * 256, 256), 256)
            wh, wl = split(w_v[lanes, :])
            igrad_v[:, lanes] = dot3(ch[...], cl[...], wh, wl, ((1,), (1,)))

    def exchange_step(s, carry):
        zs[s] = y_combined(s)
        z_copy(s, offset_of(s)).start()
        filler(s)
        return carry

    lax.fori_loop(0, NZ - 1, exchange_step, 0)
    filler(NZ - 1)
    proj_out = pltpu.make_async_copy(proj_v, proj_o, out_sem.at[0])
    igrad_out = pltpu.make_async_copy(igrad_v, igrad_o, out_sem.at[1])
    proj_out.start()
    igrad_out.start()

    def z_pair(d):
        for at in (d, d + 4):
            z_copy(0, at).wait_recv()
        return combine(zr[d - 1], zr[d + 3])

    two = z_pair(2)
    one = z_pair(1)
    three = z_pair(3)
    odd = combine(one, three)
    z_copy(0, 4).wait_recv()
    zero = combine(y_combined(NZ - 1), zr[3])
    whole = combine(combine(zero, two), odd)

    for i in range(NX):
        xs[i] = whole[8 * i : 8 * i + 8]
    x_copies = [
        remote(xs.at[(x + d) % NX], xr.at[d - 1], xs_sem.at[d - 1], xr_sem.at[d - 1], at_x(d))
        for d in range(1, NX)
    ]
    for copy in x_copies:
        copy.start()
    for copy in x_copies:
        copy.wait_recv()
    cs[...] = combine(combine(xs[x], xr[1]), combine(xr[0], xr[2]))
    c_copy = remote(cs, cr, cs_sem.at[0], cr_sem.at[0], sibling)
    c_copy.start()
    mv_copy.wait()
    mine, other = own_mv[...], sib_mv[...]
    first = c == 0
    lower, upper = jnp.where(first, mine, other), jnp.where(first, other, mine)
    moments = [jnp.concatenate([lower[i], upper[i]], axis=0) for i in range(2)]
    old_rows = w_v[pl.ds(pl.multiple_of(me // 2 * 8, 8), 8), :]
    c_copy.wait()
    summed = combine(cs[...], cr[...])
    new_rows, new_first, new_second = adam_update(summed, old_rows, moments[0], moments[1])

    half = D // 2
    mine_at = pl.multiple_of(c * half, half)
    mine_cols = pl.ds(mine_at, half)
    a_cols = pl.ds(mine_at, half // 2)
    b_cols = pl.ds(pl.multiple_of(mine_at + half // 2, half // 2), half // 2)
    wbuf[y, z, x, :, mine_cols] = jnp.where(first, new_rows[:, :half], new_rows[:, half:])

    def same(view, send, recv, target):
        return remote(view, view, send, recv, target)

    def z_block(d, target):
        zz = (z + d) % NZ
        return same(
            wbuf.at[y, zz, x, :, mine_cols], gzs_sem.at[target - 1], gzr_sem.at[target - 1],
            at_z(target),
        )

    gz = [z_block(0, d) for d in range(1, NZ)]
    for copy in gz:
        copy.start()

    new_mv[0] = jnp.where(first, new_first[:4], new_first[4:])
    new_mv[1] = jnp.where(first, new_second[:4], new_second[4:])
    m_out = pltpu.make_async_copy(new_mv.at[0], m_o, out_sem.at[2])
    v_out = pltpu.make_async_copy(new_mv.at[1], v_o, out_sem.at[3])
    m_out.start()
    v_out.start()

    for d in range(1, NZ):
        z_block(-d + NZ, d).wait_recv()

    def block(ey, ex, cols):
        return wbuf.at[(y + ey) % NY, :, (x + ex) % NX, :, cols]

    def sib_copy(ey, ex, column_start):
        cols = pl.ds(pl.multiple_of(column_start, half), half)
        return same(block(ey, ex, cols), gss_sem.at[ey, ex], gsr_sem.at[ey, ex], sibling)

    sends = []

    def start(copy):
        copy.start()
        sends.append(copy)

    for d in (2, 1, 3):
        start(same(block(0, 0, mine_cols), gxs_sem.at[d - 1], gxr_sem.at[d - 1], at_x(d)))
        start(same(block(0, 0, mine_cols), gys_sem.at[d - 1], gyr_sem.at[d - 1], at_y(d)))
    start(sib_copy(0, 0, mine_at))
    for d in (1, 3, 2):
        same(block(0, NX - d, mine_cols), gxs_sem.at[d - 1], gxr_sem.at[d - 1], at_x(d)).wait_recv()
        for e in (2, 1, 3):
            i = (d - 1) * 3 + e - 1
            start(same(block(0, NX - d, a_cols), gas_sem.at[i], gar_sem.at[i], at_y(e)))
        start(sib_copy(0, NX - d, mine_at))
        same(block(NY - d, 0, mine_cols), gys_sem.at[d - 1], gyr_sem.at[d - 1], at_y(d)).wait_recv()
        for e in (2, 1, 3):
            i = (d - 1) * 3 + e - 1
            start(same(block(NY - d, 0, b_cols), gbs_sem.at[i], gbr_sem.at[i], at_x(e)))
        start(sib_copy(NY - d, 0, mine_at))
    for d in (1, 3, 2):
        for e in (1, 3, 2):
            i = (d - 1) * 3 + e - 1
            j = (e - 1) * 3 + d - 1
            same(block(NY - e, NX - d, a_cols), gas_sem.at[i], gar_sem.at[i], at_y(e)).wait_recv()
            same(block(NY - e, NX - d, b_cols), gbs_sem.at[j], gbr_sem.at[j], at_x(d)).wait_recv()
            start(sib_copy(NY - e, NX - d, mine_at))

    other_at = (1 - c) * half
    w_outs = []
    for ey in range(NY):
        for ex in range(NX):
            sib_copy(ey, ex, other_at).wait_recv()
        plane = (y + ey) % NY
        w_out = pltpu.make_async_copy(wbuf.at[plane], w_o.at[plane], wo_sem.at[ey])
        w_out.start()
        w_outs.append(w_out)

    def drain(s, carry):
        for d in range(1, NY):
            y_copy(s, d).wait_send()
        return carry

    lax.fori_loop(0, NZ, drain, 0)
    for d in range(1, NZ):
        z_copy(0, d).wait_send()
    for copy in x_copies + gz + sends:
        copy.wait_send()
    for copy in [proj_out, igrad_out, m_out, v_out] + w_outs:
        copy.wait()


def next_kernel(tok_ref, w_ref, next_ref, copy_ref):
    th, tl = split(tok_ref[...])
    w = w_ref[...]
    wh, wl = split(w)
    copy_ref[...] = w
    part = dot3(th, tl, wh, wl, ((1,), (0,)))

    @pl.when(pl.program_id(0) == 0)
    def _():
        next_ref[...] = part

    @pl.when(pl.program_id(0) > 0)
    def _():
        next_ref[...] += part


def on_device(tokens, cotangent, weight, first_moment, second_moment):
    dma = pltpu.SemaphoreType.DMA
    any_space = pl.BlockSpec(memory_space=pl.ANY)
    rows = lambda *shape: pltpu.VMEM(shape + (D,), F32)
    projected, input_grad, gathered, new_first, new_second = pl.pallas_call(
        exchange_kernel,
        out_shape=[
            jax.ShapeDtypeStruct((T, D), F32),
            jax.ShapeDtypeStruct((T, D), F32),
            jax.ShapeDtypeStruct((NY, NZ, NX, 8, D), F32),
            jax.ShapeDtypeStruct((4, D), F32),
            jax.ShapeDtypeStruct((4, D), F32),
        ],
        in_specs=[any_space] * 5,
        out_specs=[any_space] * 5,
        scratch_shapes=[
            rows(T), rows(T), rows(D),
            pltpu.VMEM((D, T), BF16), pltpu.VMEM((D, T), BF16),
            pltpu.VMEM((T, D), BF16), pltpu.VMEM((T, D), BF16),
            pltpu.VMEM((T, D), BF16), pltpu.VMEM((T, D), BF16),
            rows(NZ, NY, CH), rows(NY - 1, NZ, CH),
            rows(NZ, CH), rows(NZ - 1, CH),
            rows(NX, 8), rows(NX - 1, 8), rows(8), rows(8),
            rows(2, 4), rows(2, 4), rows(2, 4),
            rows(NY, NZ, NX, 8), rows(T), rows(T),
            dma((5,)), dma((4,)),
            dma((NY - 1, NZ)), dma((NY - 1, NZ)), dma((NZ - 1,)), dma((NZ - 1,)),
            dma((NX - 1,)), dma((NX - 1,)), dma((2,)), dma((2,)),
            dma((NZ - 1,)), dma((NZ - 1,)), dma((NX - 1,)), dma((NX - 1,)),
            dma((NY - 1,)), dma((NY - 1,)),
            dma((9,)), dma((9,)), dma((9,)), dma((9,)),
            dma((NY, NX)), dma((NY, NX)), dma((NY,)),
        ],
        compiler_params=pltpu.CompilerParams(
            collective_id=0, has_side_effects=True, vmem_limit_bytes=48 * 2**20
        ),
        name="exchange",
    )(tokens, cotangent, weight, first_moment, second_moment)
    steps = 4
    depth = D // steps
    next_projected, new_weight = pl.pallas_call(
        next_kernel,
        grid=(steps,),
        out_shape=[jax.ShapeDtypeStruct((T, D), F32), jax.ShapeDtypeStruct((D, D), F32)],
        in_specs=[
            pl.BlockSpec((T, depth), lambda k: (0, k)),
            pl.BlockSpec((depth, D), lambda k: (k, 0)),
        ],
        out_specs=[
            pl.BlockSpec((T, D), lambda k: (0, 0)),
            pl.BlockSpec((depth, D), lambda k: (k, 0)),
        ],
        name="following",
    )(tokens, gathered.reshape(D, D))
    return (projected, input_grad, new_weight, new_first, new_second, next_projected)


def solution(mesh):
    placed = (P("dp", None), P("dp", None), P(), P("dp", None), P("dp", None))
    return jax.shard_map(
        on_device,
        mesh=mesh,
        in_specs=placed,
        out_specs=(P("dp", None), P("dp", None), P(), P("dp", None), P("dp", None), P("dp", None)),
        check_vma=False,
    )
```

```python
import jax
import jax.numpy as jnp
from jax import lax
from jax.experimental import pallas as pl
from jax.experimental.pallas import tpu as pltpu
from jax.sharding import PartitionSpec as P

beta_one = 0.9
beta_two = 0.999
rate_value = 0.01
step_count = 10
adam_epsilon = 1e-08
norm_epsilon = 1e-06

MESH = pl.DeviceIdType.MESH
NY, NZ, NX = 4, 8, 4
D = 1024
T = 256
CH = D // (NY * NZ)
F32, BF16 = jnp.float32, jnp.bfloat16


def combine(left_rows, right_rows):
    cross_term = jnp.sum(left_rows * right_rows, axis=-1, keepdims=True)
    left_norm = jnp.sum(left_rows * left_rows, axis=-1, keepdims=True)
    right_norm = jnp.sum(right_rows * right_rows, axis=-1, keepdims=True)
    left_coef = 1.0 - cross_term / (2.0 * (left_norm + norm_epsilon))
    right_coef = 1.0 - cross_term / (2.0 * (right_norm + norm_epsilon))
    return left_coef * left_rows + right_coef * right_rows


def adam_update(gradient, weight_rows, first_rows, second_rows):
    first_new = beta_one * first_rows + (1.0 - beta_one) * gradient
    second_new = beta_two * second_rows + (1.0 - beta_two) * gradient * gradient
    first_hat = first_new / (1.0 - beta_one**step_count)
    second_hat = second_new / (1.0 - beta_two**step_count)
    weight_new = weight_rows - rate_value * first_hat / (jnp.sqrt(second_hat) + adam_epsilon)
    return (weight_new, first_new, second_new)


def split(value):
    high = value.astype(BF16)
    return high, (value - high.astype(F32)).astype(BF16)


def dot(a, b, contract):
    return lax.dot_general(a, b, (contract, ((), ())), preferred_element_type=F32)


def dot3(a_high, a_low, b_high, b_low, contract):
    return (
        dot(a_high, b_high, contract)
        + dot(a_high, b_low, contract)
        + dot(a_low, b_high, contract)
    )


def offset_of(s):
    return 4 + (s + 1) // 2 * (1 - 2 * (s % 2))


def exchange_kernel(
    tok_hbm, cot_hbm, w_hbm, m_hbm, v_hbm,
    proj_v, igrad_v, next_v, wbuf, m_v, v_v,
    tok_v, cot_v, w_v, tth, ttl, th, tl, ch, cl,
    g, yr, zs, zr, xs, xr, cs, cr, own_mv, sib_mv,
    in_sem, ys_sem, yr_sem, zs_sem, zr_sem, xs_sem, xr_sem, cs_sem, cr_sem,
    gzs_sem, gzr_sem, gxs_sem, gxr_sem, gys_sem, gyr_sem,
    gas_sem, gar_sem, gbs_sem, gbr_sem, gss_sem, gsr_sem,
):
    me = lax.axis_index("dp")
    c = me % 2
    x = me // 2 % NX
    z = me // (2 * NX) % NZ
    y = me // (2 * NX * NZ)

    def device(yy, zz, xx, cc):
        return (((yy * NZ + zz) * NX + xx) * 2 + cc,)

    def at_y(d):
        return device((y + d) % NY, z, x, c)

    def at_z(d):
        return device(y, (z + d) % NZ, x, c)

    def at_x(d):
        return device(y, z, (x + d) % NX, c)

    sibling = device(y, z, x, 1 - c)

    def remote(src, dst, send, recv, target):
        return pltpu.make_async_remote_copy(
            src_ref=src, dst_ref=dst, send_sem=send, recv_sem=recv,
            device_id=target, device_id_type=MESH,
        )

    loads = [
        pltpu.make_async_copy(src, dst, in_sem.at[i])
        for i, (src, dst) in enumerate(
            [
                (tok_hbm, tok_v),
                (cot_hbm, cot_v),
                (m_hbm, own_mv.at[0]),
                (v_hbm, own_mv.at[1]),
                (w_hbm, w_v),
            ]
        )
    ]
    for load in loads:
        load.start()

    barrier = pltpu.get_barrier_semaphore()
    partners = (
        [at_y(d) for d in range(1, NY)]
        + [at_z(d) for d in range(1, NZ)]
        + [at_x(d) for d in range(1, NX)]
        + [sibling]
    )
    for partner in partners:
        pl.semaphore_signal(barrier, inc=1, device_id=partner, device_id_type=MESH)

    loads[0].wait()
    for j in range(D // 128):
        lanes = slice(128 * j, 128 * j + 128)
        piece = tok_v[:, lanes]
        th[:, lanes], tl[:, lanes] = split(piece)
        tth[lanes, :], ttl[lanes, :] = split(piece.T * (1.0 / T))
    loads[1].wait()
    for j in range(D // 256):
        lanes = slice(256 * j, 256 * j + 256)
        ch[:, lanes], cl[:, lanes] = split(cot_v[:, lanes])
    loads[2].wait()
    loads[3].wait()
    pl.semaphore_wait(barrier, len(partners))

    mv_copy = remote(own_mv, sib_mv, cs_sem.at[1], cr_sem.at[1], sibling)
    mv_copy.start()

    def y_copy(s, d):
        return remote(g.at[s, d], yr.at[d - 1, s], ys_sem.at[d - 1, s], yr_sem.at[d - 1, s], at_y(d))

    def z_copy(s, d):
        return remote(zs.at[s], zr.at[d - 1], zs_sem.at[d - 1], zr_sem.at[d - 1], at_z(d))

    def gradient_step(s, carry):
        owner = (z + offset_of(s)) % NZ
        starts = [
            pl.multiple_of((y + d) % NY * (D // NY) + owner * CH, CH) for d in range(NY)
        ]
        high = [tth[pl.ds(start, CH), :] for start in starts]
        low = [ttl[pl.ds(start, CH), :] for start in starts]
        count = NY * CH
        both = dot(jnp.concatenate(high + low, axis=0), ch[...], ((1,), (0,)))
        rest = dot(jnp.concatenate(high, axis=0), cl[...], ((1,), (0,)))
        value = both[:count] + both[count:] + rest
        for d in range(NY):
            g[s, d] = value[d * CH : (d + 1) * CH]
        for d in range(1, NY):
            y_copy(s, d).start()
        return carry

    lax.fori_loop(0, NZ, gradient_step, 0)

    loads[4].wait()

    def y_combined(s):
        for d in range(1, NY):
            y_copy(s, d).wait_recv()
        return combine(combine(g[s, 0], yr[1, s]), combine(yr[0, s], yr[2, s]))

    def filler(s):
        @pl.when(s < 4)
        def _():
            lanes = pl.ds(pl.multiple_of(s * 256, 256), 256)
            wh, wl = split(w_v[:, lanes])
            proj_v[:, lanes] = dot3(th[...], tl[...], wh, wl, ((1,), (0,)))

        @pl.when(s >= 4)
        def _():
            lanes = pl.ds(pl.multiple_of((s - 4) * 256, 256), 256)
            wh, wl = split(w_v[lanes, :])
            igrad_v[:, lanes] = dot3(ch[...], cl[...], wh, wl, ((1,), (1,)))

    def exchange_step(s, carry):
        zs[s] = y_combined(s)
        z_copy(s, offset_of(s)).start()
        filler(s)
        return carry

    lax.fori_loop(0, NZ - 1, exchange_step, 0)
    filler(NZ - 1)

    def z_pair(d):
        for at in (d, d + 4):
            z_copy(0, at).wait_recv()
        return combine(zr[d - 1], zr[d + 3])

    two = z_pair(2)
    one = z_pair(1)
    three = z_pair(3)
    odd = combine(one, three)
    z_copy(0, 4).wait_recv()
    zero = combine(y_combined(NZ - 1), zr[3])
    whole = combine(combine(zero, two), odd)

    for i in range(NX):
        xs[i] = whole[8 * i : 8 * i + 8]
    x_copies = [
        remote(xs.at[(x + d) % NX], xr.at[d - 1], xs_sem.at[d - 1], xr_sem.at[d - 1], at_x(d))
        for d in range(1, NX)
    ]
    for copy in x_copies:
        copy.start()
    for copy in x_copies:
        copy.wait_recv()
    cs[...] = combine(combine(xs[x], xr[1]), combine(xr[0], xr[2]))
    c_copy = remote(cs, cr, cs_sem.at[0], cr_sem.at[0], sibling)
    c_copy.start()
    mv_copy.wait()
    mine, other = own_mv[...], sib_mv[...]
    first = c == 0
    lower, upper = jnp.where(first, mine, other), jnp.where(first, other, mine)
    moments = [jnp.concatenate([lower[i], upper[i]], axis=0) for i in range(2)]
    old_rows = w_v[pl.ds(pl.multiple_of(me // 2 * 8, 8), 8), :]
    c_copy.wait()
    summed = combine(cs[...], cr[...])
    new_rows, new_first, new_second = adam_update(summed, old_rows, moments[0], moments[1])

    half = D // 2
    mine_at = pl.multiple_of(c * half, half)
    mine_cols = pl.ds(mine_at, half)
    a_cols = pl.ds(mine_at, half // 2)
    b_cols = pl.ds(pl.multiple_of(mine_at + half // 2, half // 2), half // 2)
    wbuf[y, z, x, :, mine_cols] = jnp.where(first, new_rows[:, :half], new_rows[:, half:])

    def same(view, send, recv, target):
        return remote(view, view, send, recv, target)

    def z_block(d, target):
        zz = (z + d) % NZ
        return same(
            wbuf.at[y, zz, x, :, mine_cols], gzs_sem.at[target - 1], gzr_sem.at[target - 1],
            at_z(target),
        )

    gz = [z_block(0, d) for d in range(1, NZ)]
    for copy in gz:
        copy.start()

    m_v[...] = jnp.where(first, new_first[:4], new_first[4:])
    v_v[...] = jnp.where(first, new_second[:4], new_second[4:])

    for d in range(1, NZ):
        z_block(-d + NZ, d).wait_recv()

    def block(ey, ex, cols):
        return wbuf.at[(y + ey) % NY, :, (x + ex) % NX, :, cols]

    def sib_copy(ey, ex, column_start):
        cols = pl.ds(pl.multiple_of(column_start, half), half)
        return same(block(ey, ex, cols), gss_sem.at[ey, ex], gsr_sem.at[ey, ex], sibling)

    sends = []

    def start(copy):
        copy.start()
        sends.append(copy)

    for d in (2, 1, 3):
        start(same(block(0, 0, mine_cols), gxs_sem.at[d - 1], gxr_sem.at[d - 1], at_x(d)))
        start(same(block(0, 0, mine_cols), gys_sem.at[d - 1], gyr_sem.at[d - 1], at_y(d)))
    start(sib_copy(0, 0, mine_at))
    for d in (1, 3, 2):
        same(block(0, NX - d, mine_cols), gxs_sem.at[d - 1], gxr_sem.at[d - 1], at_x(d)).wait_recv()
        for e in (2, 1, 3):
            i = (d - 1) * 3 + e - 1
            start(same(block(0, NX - d, a_cols), gas_sem.at[i], gar_sem.at[i], at_y(e)))
        start(sib_copy(0, NX - d, mine_at))
        same(block(NY - d, 0, mine_cols), gys_sem.at[d - 1], gyr_sem.at[d - 1], at_y(d)).wait_recv()
        for e in (2, 1, 3):
            i = (d - 1) * 3 + e - 1
            start(same(block(NY - d, 0, b_cols), gbs_sem.at[i], gbr_sem.at[i], at_x(e)))
        start(sib_copy(NY - d, 0, mine_at))
    for d in (1, 3, 2):
        for e in (1, 3, 2):
            i = (d - 1) * 3 + e - 1
            j = (e - 1) * 3 + d - 1
            same(block(NY - e, NX - d, a_cols), gas_sem.at[i], gar_sem.at[i], at_y(e)).wait_recv()
            same(block(NY - e, NX - d, b_cols), gbs_sem.at[j], gbr_sem.at[j], at_x(d)).wait_recv()
            start(sib_copy(NY - e, NX - d, mine_at))

    other_at = (1 - c) * half
    def following(ey):
        plane = (y + ey) % NY
        lanes = pl.ds(pl.multiple_of(plane * (D // NY), D // NY), D // NY)
        wh, wl = split(wbuf[plane].reshape(D // NY, D))
        return dot3(th[:, lanes], tl[:, lanes], wh, wl, ((1,), (0,)))

    for ey in range(NY):
        for ex in range(NX):
            sib_copy(ey, ex, other_at).wait_recv()
        if ey == 0:
            next_v[...] = following(ey)
        else:
            next_v[...] += following(ey)

    def drain(s, carry):
        for d in range(1, NY):
            y_copy(s, d).wait_send()
        return carry

    lax.fori_loop(0, NZ, drain, 0)
    for d in range(1, NZ):
        z_copy(0, d).wait_send()
    for copy in x_copies + gz + sends:
        copy.wait_send()


PIECES = (2, 2, 2, 4, 1, 1)


def store_kernel(*refs):
    sources, targets, sem = refs[:6], refs[6:12], refs[12]
    copies = []
    for i, (source, target) in enumerate(zip(sources, targets)):
        count = PIECES[i]
        size = source.shape[0] // count
        for j in range(count):
            rows = pl.ds(j * size, size)
            copies.append(pltpu.make_async_copy(source.at[rows], target.at[rows], sem.at[len(copies)]))
    for copy in copies:
        copy.start()
    for copy in copies:
        copy.wait()


def on_device(tokens, cotangent, weight, first_moment, second_moment):
    dma = pltpu.SemaphoreType.DMA
    any_space = pl.BlockSpec(memory_space=pl.ANY)
    rows = lambda *shape: pltpu.VMEM(shape + (D,), F32)
    shapes = [(T, D), (T, D), (T, D), (NY, NZ, NX, 8, D), (4, D), (4, D)]
    held = pl.pallas_call(
        exchange_kernel,
        out_shape=[pltpu.VMEM(shape, F32) for shape in shapes],
        in_specs=[any_space] * 5,
        out_specs=[pl.BlockSpec(memory_space=pltpu.VMEM)] * 6,
        scratch_shapes=[
            rows(T), rows(T), rows(D),
            pltpu.VMEM((D, T), BF16), pltpu.VMEM((D, T), BF16),
            pltpu.VMEM((T, D), BF16), pltpu.VMEM((T, D), BF16),
            pltpu.VMEM((T, D), BF16), pltpu.VMEM((T, D), BF16),
            rows(NZ, NY, CH), rows(NY - 1, NZ, CH),
            rows(NZ, CH), rows(NZ - 1, CH),
            rows(NX, 8), rows(NX - 1, 8), rows(8), rows(8),
            rows(2, 4), rows(2, 4),
            dma((5,)),
            dma((NY - 1, NZ)), dma((NY - 1, NZ)), dma((NZ - 1,)), dma((NZ - 1,)),
            dma((NX - 1,)), dma((NX - 1,)), dma((2,)), dma((2,)),
            dma((NZ - 1,)), dma((NZ - 1,)), dma((NX - 1,)), dma((NX - 1,)),
            dma((NY - 1,)), dma((NY - 1,)),
            dma((9,)), dma((9,)), dma((9,)), dma((9,)),
            dma((NY, NX)), dma((NY, NX)),
        ],
        compiler_params=pltpu.CompilerParams(
            collective_id=0, has_side_effects=True, vmem_limit_bytes=52 * 2**20
        ),
        name="exchange",
    )(tokens, cotangent, weight, first_moment, second_moment)
    projected, input_grad, next_projected, new_weight, new_first, new_second = pl.pallas_call(
        store_kernel,
        out_shape=[jax.ShapeDtypeStruct(shape, F32) for shape in shapes],
        in_specs=[any_space] * 6,
        out_specs=[pl.BlockSpec(memory_space=pltpu.HBM)] * 6,
        scratch_shapes=[dma((sum(PIECES),))],
        compiler_params=pltpu.CompilerParams(vmem_limit_bytes=2**20),
        name="store",
    )(*held)
    new_weight = new_weight.reshape(D, D)
    return (projected, input_grad, new_weight, new_first, new_second, next_projected)


def solution(mesh):
    placed = (P("dp", None), P("dp", None), P(), P("dp", None), P("dp", None))
    return jax.shard_map(
        on_device,
        mesh=mesh,
        in_specs=placed,
        out_specs=(P("dp", None), P("dp", None), P(), P("dp", None), P("dp", None), P("dp", None)),
        check_vma=False,
    )
```

```python
import jax
import jax.numpy as jnp
from jax import lax
from jax.experimental import pallas as pl
from jax.experimental.pallas import tpu as pltpu
from jax.sharding import PartitionSpec as P

beta_one = 0.9
beta_two = 0.999
rate_value = 0.01
step_count = 10
adam_epsilon = 1e-08
norm_epsilon = 1e-06

MESH = pl.DeviceIdType.MESH
NY, NZ, NX = 4, 8, 4
D = 1024
T = 256
CH = D // (NY * NZ)
FAR = (2, 1, 3)
F32, BF16 = jnp.float32, jnp.bfloat16


def combine(left_rows, right_rows):
    cross_term = jnp.sum(left_rows * right_rows, axis=-1, keepdims=True)
    left_norm = jnp.sum(left_rows * left_rows, axis=-1, keepdims=True)
    right_norm = jnp.sum(right_rows * right_rows, axis=-1, keepdims=True)
    left_coef = 1.0 - cross_term / (2.0 * (left_norm + norm_epsilon))
    right_coef = 1.0 - cross_term / (2.0 * (right_norm + norm_epsilon))
    return left_coef * left_rows + right_coef * right_rows


def adam_update(gradient, weight_rows, first_rows, second_rows):
    first_new = beta_one * first_rows + (1.0 - beta_one) * gradient
    second_new = beta_two * second_rows + (1.0 - beta_two) * gradient * gradient
    first_hat = first_new / (1.0 - beta_one**step_count)
    second_hat = second_new / (1.0 - beta_two**step_count)
    weight_new = weight_rows - rate_value * first_hat / (jnp.sqrt(second_hat) + adam_epsilon)
    return (weight_new, first_new, second_new)


def split(value):
    high = value.astype(BF16)
    return high, (value - high.astype(F32)).astype(BF16)


def dot(a, b, contract):
    return lax.dot_general(a, b, (contract, ((), ())), preferred_element_type=F32)


def dot3(a_high, a_low, b_high, b_low, contract):
    return (
        dot(a_high, b_high, contract)
        + dot(a_high, b_low, contract)
        + dot(a_low, b_high, contract)
    )


def offset_of(s):
    return 4 + (s + 1) // 2 * (1 - 2 * (s % 2))


def exchange_kernel(
    tok_hbm, cot_hbm, w_hbm, m_hbm, v_hbm,
    proj_v, igrad_v, next_v, wbuf, m_v, v_v,
    tok_v, cot_v, w_v, tth, ttl, th, tl, ch, cl,
    g, yr, zs, zr, zz, xs, xr, cs, cr, own_mv, sib_mv,
    in_sem, ys_sem, yr_sem, zs_sem, zr_sem, xs_sem, xr_sem, cs_sem, cr_sem,
    gzs_sem, gzr_sem, gns_sem, gnr_sem, g2s_sem, g2r_sem, fis_sem, fir_sem, fzs_sem, fzr_sem,
    gas_sem, gar_sem, gbs_sem, gbr_sem, gss_sem, gsr_sem,
):
    me = lax.axis_index("dp")
    c = me % 2
    x = me // 2 % NX
    z = me // (2 * NX) % NZ
    y = me // (2 * NX * NZ)

    def device(yy, zz, xx, cc):
        return (((yy * NZ + zz) * NX + xx) * 2 + cc,)

    def at_y(d):
        return device((y + d) % NY, z, x, c)

    def at_z(d):
        return device(y, (z + d) % NZ, x, c)

    def at_x(d):
        return device(y, z, (x + d) % NX, c)

    sibling = device(y, z, x, 1 - c)

    def far(ex):
        return device((y + 2) % NY, z, (x + ex) % NX, c)

    def remote(src, dst, send, recv, target):
        return pltpu.make_async_remote_copy(
            src_ref=src, dst_ref=dst, send_sem=send, recv_sem=recv,
            device_id=target, device_id_type=MESH,
        )

    loads = [
        pltpu.make_async_copy(src, dst, in_sem.at[i])
        for i, (src, dst) in enumerate(
            [
                (tok_hbm, tok_v),
                (cot_hbm, cot_v),
                (m_hbm, own_mv.at[0]),
                (v_hbm, own_mv.at[1]),
                (w_hbm, w_v),
            ]
        )
    ]
    for load in loads:
        load.start()

    barrier = pltpu.get_barrier_semaphore()
    partners = (
        [at_y(d) for d in range(1, NY)]
        + [at_z(d) for d in range(1, NZ)]
        + [at_x(d) for d in range(1, NX)]
        + [far(ex) for ex in FAR]
        + [sibling]
    )
    for partner in partners:
        pl.semaphore_signal(barrier, inc=1, device_id=partner, device_id_type=MESH)

    loads[0].wait()
    for j in range(D // 128):
        lanes = slice(128 * j, 128 * j + 128)
        piece = tok_v[:, lanes]
        th[:, lanes], tl[:, lanes] = split(piece)
        tth[lanes, :], ttl[lanes, :] = split(piece.T * (1.0 / T))
    loads[1].wait()
    for j in range(D // 256):
        lanes = slice(256 * j, 256 * j + 256)
        ch[:, lanes], cl[:, lanes] = split(cot_v[:, lanes])
    loads[2].wait()
    loads[3].wait()
    pl.semaphore_wait(barrier, len(partners))

    mv_copy = remote(own_mv, sib_mv, cs_sem.at[1], cr_sem.at[1], sibling)
    mv_copy.start()

    def y_copy(s, d):
        return remote(g.at[s, d], yr.at[d - 1, s], ys_sem.at[d - 1, s], yr_sem.at[d - 1, s], at_y(d))

    def z_copy(s, d):
        return remote(zs.at[s], zr.at[d - 1], zs_sem.at[d - 1], zr_sem.at[d - 1], at_z(d))

    def gradient_step(s, carry):
        owner = (z + offset_of(s)) % NZ
        starts = [
            pl.multiple_of((y + d) % NY * (D // NY) + owner * CH, CH) for d in range(NY)
        ]
        high = [tth[pl.ds(start, CH), :] for start in starts]
        low = [ttl[pl.ds(start, CH), :] for start in starts]
        count = NY * CH
        both = dot(jnp.concatenate(high + low, axis=0), ch[...], ((1,), (0,)))
        rest = dot(jnp.concatenate(high, axis=0), cl[...], ((1,), (0,)))
        value = both[:count] + both[count:] + rest
        for d in range(NY):
            g[s, d] = value[d * CH : (d + 1) * CH]
        for d in range(1, NY):
            y_copy(s, d).start()
        return carry

    lax.fori_loop(0, NZ, gradient_step, 0)

    loads[4].wait()

    def y_combined(s):
        for d in range(1, NY):
            y_copy(s, d).wait_recv()
        return combine(combine(g[s, 0], yr[1, s]), combine(yr[0, s], yr[2, s]))

    def filler(s):
        @pl.when(s < 4)
        def _():
            lanes = pl.ds(pl.multiple_of(s * 256, 256), 256)
            wh, wl = split(w_v[:, lanes])
            proj_v[:, lanes] = dot3(th[...], tl[...], wh, wl, ((1,), (0,)))

        @pl.when(s >= 4)
        def _():
            lanes = pl.ds(pl.multiple_of((s - 4) * 256, 256), 256)
            wh, wl = split(w_v[lanes, :])
            igrad_v[:, lanes] = dot3(ch[...], cl[...], wh, wl, ((1,), (1,)))

    def exchange_step(s, carry):
        zs[s] = y_combined(s)
        z_copy(s, offset_of(s)).start()
        filler(s)
        return carry

    lax.fori_loop(0, NZ - 1, exchange_step, 0)
    filler(NZ - 1)

    def z_pair(d):
        for at in (d, d + 4):
            z_copy(0, at).wait_recv()
        return combine(zr[d - 1], zr[d + 3])

    two = z_pair(2)
    one = z_pair(1)
    three = z_pair(3)
    odd = combine(one, three)
    zz[0], zz[1] = two, odd
    z_copy(0, 4).wait_recv()
    for d in range(1, NY):
        y_copy(NZ - 1, d).wait_recv()
    x_copies = []
    for d in (2, 1, 3, 0):
        at = pl.ds(pl.multiple_of((x + d) % NX * 8, 8), 8)
        last = NZ - 1
        across = combine(g[last, 0, at], yr[1, last, at])
        across = combine(across, combine(yr[0, last, at], yr[2, last, at]))
        across = combine(combine(across, zr[3, at]), zz[0, at])
        xs[d] = combine(across, zz[1, at])
        if d > 0:
            copy = remote(xs.at[d], xr.at[d - 1], xs_sem.at[d - 1], xr_sem.at[d - 1], at_x(d))
            copy.start()
            x_copies.append(copy)
    for copy in x_copies:
        copy.wait_recv()
    cs[...] = combine(combine(xs[0], xr[1]), combine(xr[0], xr[2]))
    c_copy = remote(cs, cr, cs_sem.at[0], cr_sem.at[0], sibling)
    c_copy.start()
    mv_copy.wait()
    mine, other = own_mv[...], sib_mv[...]
    first = c == 0
    lower, upper = jnp.where(first, mine, other), jnp.where(first, other, mine)
    moments = [jnp.concatenate([lower[i], upper[i]], axis=0) for i in range(2)]
    old_rows = w_v[pl.ds(pl.multiple_of(me // 2 * 8, 8), 8), :]
    c_copy.wait()
    summed = combine(cs[...], cr[...])
    new_rows, new_first, new_second = adam_update(summed, old_rows, moments[0], moments[1])

    half = D // 2
    mine_at = pl.multiple_of(c * half, half)
    mine_cols = pl.ds(mine_at, half)
    a_cols = pl.ds(mine_at, half // 2)
    b_cols = pl.ds(pl.multiple_of(mine_at + half // 2, half // 2), half // 2)

    wbuf[y, z, x, :, mine_cols] = jnp.where(first, new_rows[:, :half], new_rows[:, half:])

    def same(view, send, recv, target):
        return remote(view, view, send, recv, target)

    def z_block(d, target):
        view = wbuf.at[y, (z + d) % NZ, x, :, mine_cols]
        return same(view, gzs_sem.at[target - 1], gzr_sem.at[target - 1], at_z(target))

    sends = []

    def start(copy):
        copy.start()
        sends.append(copy)

    neighbours = [at_x(1), at_x(3), at_y(1), at_y(3)]

    def to_neighbours(d):
        view = wbuf.at[y, (z + d) % NZ, x, :, mine_cols]
        for i, target in enumerate(neighbours):
            same(view, gns_sem.at[i], gnr_sem.at[i], target).start()

    far_order = (4, 3, 5, 2, 6, 1, 7)
    for d in far_order:
        start(z_block(0, d))
    to_neighbours(0)
    for j, ex in enumerate(FAR):
        start(same(wbuf.at[y, z, x, :, mine_cols], fis_sem.at[j], fir_sem.at[j], far(ex)))

    m_v[...] = jnp.where(first, new_first[:4], new_first[4:])
    v_v[...] = jnp.where(first, new_second[:4], new_second[4:])

    for d in (1, 7, 2, 6, 3, 5, 4):
        z_block(NZ - d, d).wait_recv()
        to_neighbours(NZ - d)

    def block(ey, ex, cols):
        return wbuf.at[(y + ey) % NY, :, (x + ex) % NX, :, cols]

    def sib_copy(ey, ex, column_start):
        cols = pl.ds(pl.multiple_of(column_start, half), half)
        return same(block(ey, ex, cols), gss_sem.at[ey, ex], gsr_sem.at[ey, ex], sibling)

    def far_block(j, d):
        return wbuf.at[(y + 2) % NY, (z + d) % NZ, (x + NX - FAR[j]) % NX, :, mine_cols]

    def far_copy(j, at, d):
        i = j * (NZ - 1) + d - 1
        return same(far_block(j, at), fzs_sem.at[i], fzr_sem.at[i], at_z(d))

    def two_away(i, ey, ex):
        target = at_x(2) if i == 0 else at_y(2)
        return same(block(ey, ex, mine_cols), g2s_sem.at[i], g2r_sem.at[i], target)

    order = [3, 1, 2]

    def from_neighbour(i):
        ey, ex = [(0, 3), (0, 1), (3, 0), (1, 0)][i]
        return same(block(ey, ex, mine_cols), gns_sem.at[i], gnr_sem.at[i], neighbours[i])

    def a_flow(k, direction, ey):
        i = 2 * k + direction
        return same(block(ey, order[k], a_cols), gas_sem.at[i], gar_sem.at[i], neighbours[2 + direction])

    def b_flow(k, target, ex):
        i = 3 * k + target
        return same(
            block(order[k], ex, b_cols), gbs_sem.at[i], gbr_sem.at[i], at_x((1, 3, 2)[target])
        )

    start(two_away(0, 0, 0))
    start(two_away(1, 0, 0))
    for j in range(3):
        same(far_block(j, 0), fis_sem.at[j], fir_sem.at[j], far(FAR[j])).wait_recv()
        for d in far_order:
            start(far_copy(j, 0, d))
    start(sib_copy(0, 0, mine_at))
    for k in range(2):
        from_neighbour(2 + k).wait_recv()
        for target in (2, 0, 1):
            start(b_flow(k, target, 0))
        start(sib_copy(order[k], 0, mine_at))
        from_neighbour(k).wait_recv()
        for direction in range(2):
            start(a_flow(k, direction, 0))
        start(sib_copy(0, order[k], mine_at))
    two_away(0, 0, 2).wait_recv()
    for direction in range(2):
        start(a_flow(2, direction, 0))
    start(sib_copy(0, 2, mine_at))
    two_away(1, 2, 0).wait_recv()
    start(sib_copy(2, 0, mine_at))

    other_at = (1 - c) * half

    def following(ey):
        for ex in range(NX):
            sib_copy(ey, ex, other_at).wait_recv()
        plane = (y + ey) % NY
        lanes = pl.ds(pl.multiple_of(plane * (D // NY), D // NY), D // NY)
        wh, wl = split(wbuf[plane].reshape(D // NY, D))
        return dot3(th[:, lanes], tl[:, lanes], wh, wl, ((1,), (0,)))

    for j in range(3):
        for d in far_order:
            far_copy(j, NZ - d, d).wait_recv()
        start(sib_copy(2, NX - FAR[j], mine_at))
    next_v[...] = following(0)
    for k in range(2):
        for direction in range(2):
            a_flow(k, direction, order[direction]).wait_recv()
            b_flow(direction, k, order[k]).wait_recv()
            start(sib_copy(order[direction], order[k], mine_at))
    for direction in range(2):
        a_flow(2, direction, order[direction]).wait_recv()
        b_flow(direction, 2, 2).wait_recv()
        start(sib_copy(order[direction], 2, mine_at))
    for ey in (2, 1, 3):
        next_v[...] += following(ey)

    def drain(s, carry):
        for d in range(1, NY):
            y_copy(s, d).wait_send()
        return carry

    lax.fori_loop(0, NZ, drain, 0)
    for d in range(1, NZ):
        z_copy(0, d).wait_send()
    for i in range(4):
        from_neighbour(i).wait_send()
    for copy in x_copies + sends:
        copy.wait_send()


PIECES = (2, 2, 2, 4, 1, 1)


def store_kernel(*refs):
    sources, targets, sem = refs[:6], refs[6:12], refs[12]
    copies = []
    for i, (source, target) in enumerate(zip(sources, targets)):
        count = PIECES[i]
        size = source.shape[0] // count
        for j in range(count):
            rows = pl.ds(j * size, size)
            copies.append(pltpu.make_async_copy(source.at[rows], target.at[rows], sem.at[len(copies)]))
    for copy in copies:
        copy.start()
    for copy in copies:
        copy.wait()


def on_device(tokens, cotangent, weight, first_moment, second_moment):
    dma = pltpu.SemaphoreType.DMA
    any_space = pl.BlockSpec(memory_space=pl.ANY)
    rows = lambda *shape: pltpu.VMEM(shape + (D,), F32)
    shapes = [(T, D), (T, D), (T, D), (NY, NZ, NX, 8, D), (4, D), (4, D)]
    held = pl.pallas_call(
        exchange_kernel,
        out_shape=[pltpu.VMEM(shape, F32) for shape in shapes],
        in_specs=[any_space] * 5,
        out_specs=[pl.BlockSpec(memory_space=pltpu.VMEM)] * 6,
        scratch_shapes=[
            rows(T), rows(T), rows(D),
            pltpu.VMEM((D, T), BF16), pltpu.VMEM((D, T), BF16),
            pltpu.VMEM((T, D), BF16), pltpu.VMEM((T, D), BF16),
            pltpu.VMEM((T, D), BF16), pltpu.VMEM((T, D), BF16),
            rows(NZ, NY, CH), rows(NY - 1, NZ, CH),
            rows(NZ, CH), rows(NZ - 1, CH), rows(2, CH),
            rows(NX, 8), rows(NX - 1, 8), rows(8), rows(8),
            rows(2, 4), rows(2, 4),
            dma((5,)),
            dma((NY - 1, NZ)), dma((NY - 1, NZ)), dma((NZ - 1,)), dma((NZ - 1,)),
            dma((NX - 1,)), dma((NX - 1,)), dma((2,)), dma((2,)),
            dma((NZ - 1,)), dma((NZ - 1,)), dma((4,)), dma((4,)), dma((2,)), dma((2,)),
            dma((3,)), dma((3,)), dma((3 * (NZ - 1),)), dma((3 * (NZ - 1),)),
            dma((6,)), dma((6,)), dma((6,)), dma((6,)),
            dma((NY, NX)), dma((NY, NX)),
        ],
        compiler_params=pltpu.CompilerParams(
            collective_id=0, has_side_effects=True, vmem_limit_bytes=52 * 2**20
        ),
        name="exchange",
    )(tokens, cotangent, weight, first_moment, second_moment)
    projected, input_grad, next_projected, new_weight, new_first, new_second = pl.pallas_call(
        store_kernel,
        out_shape=[jax.ShapeDtypeStruct(shape, F32) for shape in shapes],
        in_specs=[any_space] * 6,
        out_specs=[pl.BlockSpec(memory_space=pltpu.HBM)] * 6,
        scratch_shapes=[dma((sum(PIECES),))],
        compiler_params=pltpu.CompilerParams(vmem_limit_bytes=2**20),
        name="store",
    )(*held)
    new_weight = new_weight.reshape(D, D)
    return (projected, input_grad, new_weight, new_first, new_second, next_projected)


def solution(mesh):
    placed = (P("dp", None), P("dp", None), P(), P("dp", None), P("dp", None))
    return jax.shard_map(
        on_device,
        mesh=mesh,
        in_specs=placed,
        out_specs=(P("dp", None), P("dp", None), P(), P("dp", None), P("dp", None), P("dp", None)),
        check_vma=False,
    )
```

```python
import jax
import jax.numpy as jnp
from jax import lax
from jax.experimental import pallas as pl
from jax.experimental.pallas import tpu as pltpu
from jax.sharding import PartitionSpec as P

beta_one = 0.9
beta_two = 0.999
rate_value = 0.01
step_count = 10
adam_epsilon = 1e-08
norm_epsilon = 1e-06

MESH = pl.DeviceIdType.MESH
NY, NZ, NX = 4, 8, 4
D = 1024
T = 256
CH = D // (NY * NZ)
FAR = (2, 1, 3)
SIDE = 256
F32, BF16 = jnp.float32, jnp.bfloat16


def combine(left_rows, right_rows):
    cross_term = jnp.sum(left_rows * right_rows, axis=-1, keepdims=True)
    left_norm = jnp.sum(left_rows * left_rows, axis=-1, keepdims=True)
    right_norm = jnp.sum(right_rows * right_rows, axis=-1, keepdims=True)
    left_coef = 1.0 - cross_term / (2.0 * (left_norm + norm_epsilon))
    right_coef = 1.0 - cross_term / (2.0 * (right_norm + norm_epsilon))
    return left_coef * left_rows + right_coef * right_rows


def adam_update(gradient, weight_rows, first_rows, second_rows):
    first_new = beta_one * first_rows + (1.0 - beta_one) * gradient
    second_new = beta_two * second_rows + (1.0 - beta_two) * gradient * gradient
    first_hat = first_new / (1.0 - beta_one**step_count)
    second_hat = second_new / (1.0 - beta_two**step_count)
    weight_new = weight_rows - rate_value * first_hat / (jnp.sqrt(second_hat) + adam_epsilon)
    return (weight_new, first_new, second_new)


def split(value):
    high = value.astype(BF16)
    return high, (value - high.astype(F32)).astype(BF16)


def dot(a, b, contract):
    return lax.dot_general(a, b, (contract, ((), ())), preferred_element_type=F32)


def dot3(a_high, a_low, b_high, b_low, contract):
    return (
        dot(a_high, b_high, contract)
        + dot(a_high, b_low, contract)
        + dot(a_low, b_high, contract)
    )


def offset_of(s):
    return 4 + (s + 1) // 2 * (1 - 2 * (s % 2))


def exchange_kernel(
    tok_hbm, cot_hbm, w_hbm, m_hbm, v_hbm,
    proj_v, igrad_v, next_v, wbuf, m_v, v_v,
    tok_v, cot_v, w_v, tth, ttl, ttp, th, tl, thp, tlp, ch, cl,
    g, yr, zs, zr, zz, xs, xr, cs, cr, own_mv, sib_mv,
    in_sem, ys_sem, yr_sem, zs_sem, zr_sem, xs_sem, xr_sem, cs_sem, cr_sem,
    gzs_sem, gzr_sem, gxs_sem, gxr_sem, gys_sem, gyr_sem, gns_sem, gnr_sem, g2s_sem, g2r_sem,
    y0s_sem, y0r_sem, fis_sem, fir_sem, fzs_sem, fzr_sem, gas_sem, gar_sem, gbs_sem, gbr_sem, gss_sem, gsr_sem,
):
    me = lax.axis_index("dp")
    c = me % 2
    x = me // 2 % NX
    z = me // (2 * NX) % NZ
    y = me // (2 * NX * NZ)
    odd = x % 2 == 1
    even = x % 2 == 0
    owns = [even, odd]
    others = [odd, even]

    def device(yy, zz, xx, cc):
        return (((yy * NZ + zz) * NX + xx) * 2 + cc,)

    def at_y(d):
        return device((y + d) % NY, z, x, c)

    def at_z(d):
        return device(y, (z + d) % NZ, x, c)

    def at_x(d):
        return device(y, z, (x + d) % NX, c)

    sibling = device(y, z, x, 1 - c)

    def far(ex):
        return device((y + 2) % NY, z, (x + ex) % NX, c)

    def remote(src, dst, send, recv, target):
        return pltpu.make_async_remote_copy(
            src_ref=src, dst_ref=dst, send_sem=send, recv_sem=recv,
            device_id=target, device_id_type=MESH,
        )

    loads = [
        pltpu.make_async_copy(src, dst, in_sem.at[i])
        for i, (src, dst) in enumerate(
            [
                (tok_hbm, tok_v),
                (cot_hbm, cot_v),
                (m_hbm, own_mv.at[0]),
                (v_hbm, own_mv.at[1]),
                (w_hbm, w_v),
            ]
        )
    ]
    for load in loads:
        load.start()

    barrier = pltpu.get_barrier_semaphore()
    partners = (
        [at_y(d) for d in range(1, NY)]
        + [at_z(d) for d in range(1, NZ)]
        + [at_x(d) for d in range(1, NX)]
        + [far(ex) for ex in FAR]
        + [sibling]
    )
    for partner in partners:
        pl.semaphore_signal(barrier, inc=1, device_id=partner, device_id_type=MESH)

    loads[0].wait()
    for j in range(D // 128):
        lanes = slice(128 * j, 128 * j + 128)
        piece = tok_v[:, lanes]
        th[:, lanes], tl[:, lanes] = split(piece)
        turned = piece.T
        tth[lanes, :], ttl[lanes, :] = split(turned * (1.0 / T))
        turned = turned.reshape(4, NX, 8, T)
        plane, quarter = j // 2, j % 2
        for b in range(2):
            at = (2 * b + plane % 2) * 256 + plane // 2 * 128 + quarter * 64
            ttp[at : at + 64] = jnp.stack([turned[:, b], turned[:, b + 2]], axis=1).reshape(64, T)
    loads[1].wait()
    for j in range(D // 256):
        lanes = slice(256 * j, 256 * j + 256)
        ch[:, lanes], cl[:, lanes] = split(cot_v[:, lanes])
    loads[2].wait()
    loads[3].wait()
    pl.semaphore_wait(barrier, len(partners))

    mv_copy = remote(own_mv, sib_mv, cs_sem.at[1], cr_sem.at[1], sibling)
    mv_copy.start()

    def y_copy(b, s, d):
        rows = pl.ds(2 * b, 2)
        return remote(
            g.at[s, d, rows], yr.at[d - 1, s, rows],
            ys_sem.at[b, d - 1, s], yr_sem.at[b, d - 1, s], at_y(d),
        )

    def z_copy(b, s, d):
        rows = pl.ds(2 * b, 2)
        return remote(
            zs.at[s, rows], zr.at[d - 1, rows], zs_sem.at[b, d - 1], zr_sem.at[b, d - 1], at_z(d)
        )

    def gradient_step(s, carry):
        owner = (z + offset_of(s)) % NZ
        starts = [
            pl.multiple_of((y + d) % NY * (D // NY) + owner * CH, CH) for d in range(NY)
        ]
        high = [tth[pl.ds(start, CH), :] for start in starts]
        low = [ttl[pl.ds(start, CH), :] for start in starts]
        count = NY * CH
        both = dot(jnp.concatenate(high + low, axis=0), ch[...], ((1,), (0,)))
        rest = dot(jnp.concatenate(high, axis=0), cl[...], ((1,), (0,)))
        value = both[:count] + both[count:] + rest
        for d in range(NY):
            for i in range(NX):
                at = d * CH + 8 * i
                g[s, d, 2 * (i % 2) + i // 2] = value[at : at + 8]
        for d in (2, 1, 3):
            y_copy(0, s, d).start()
        return carry

    lax.fori_loop(0, NZ, gradient_step, 0)

    def second_sends(s, carry):
        for d in (2, 1, 3):
            y_copy(1, s, d).start()
        return carry

    lax.fori_loop(0, NZ, second_sends, 0)

    loads[4].wait()

    def y_step(b, s):
        for d in range(1, NY):
            y_copy(b, s, d).wait_recv()
        rows = pl.ds(2 * b, 2)
        across = combine(g[s, 0, rows], yr[1, s, rows])
        zs[s, rows] = combine(across, combine(yr[0, s, rows], yr[2, s, rows]))
        z_copy(b, s, offset_of(s)).start()

    def filler(s):
        @pl.when(s < 4)
        def _():
            lanes = pl.ds(pl.multiple_of(s * 256, 256), 256)
            wh, wl = split(w_v[:, lanes])
            proj_v[:, lanes] = dot3(th[...], tl[...], wh, wl, ((1,), (0,)))

        @pl.when(s >= 4)
        def _():
            lanes = pl.ds(pl.multiple_of((s - 4) * 256, 256), 256)
            wh, wl = split(w_v[lanes, :])
            igrad_v[:, lanes] = dot3(ch[...], cl[...], wh, wl, ((1,), (1,)))

    def first_step(s, carry):
        y_step(0, s)
        filler(s)
        return carry

    lax.fori_loop(0, NZ - 1, first_step, 0)

    def z_pair(b, d):
        for at in (d, d + 4):
            z_copy(b, 0, at).wait_recv()
        rows = pl.ds(2 * b, 2)
        return combine(zr[d - 1, rows], zr[d + 3, rows])

    def x_copy(b, d):
        return remote(
            xs.at[b, d], xr.at[b, d - 1], xs_sem.at[b, d - 1], xr_sem.at[b, d - 1], at_x(d)
        )

    def reduce_sends(b):
        zz[b, 0] = z_pair(b, 2)
        zz[b, 1] = combine(z_pair(b, 1), z_pair(b, 3))
        z_copy(b, 0, 4).wait_recv()
        last = NZ - 1
        for d in range(1, NY):
            y_copy(b, last, d).wait_recv()

        def piece(d):
            h = (x + d) % NX // 2
            q = 2 * b + h
            across = combine(g[last, 0, q], yr[1, last, q])
            across = combine(across, combine(yr[0, last, q], yr[2, last, q]))
            across = combine(combine(across, zr[3, q]), zz[b, 0, h])
            xs[b, d] = combine(across, zz[b, 1, h])

        @pl.when(owns[b])
        def _():
            piece(2)
            x_copy(b, 2).start()
            piece(0)

        @pl.when(others[b])
        def _():
            for d in (1, 3):
                piece(d)
                x_copy(b, d).start()

    c_copy = remote(cs, cr, cs_sem.at[0], cr_sem.at[0], sibling)

    def gather_rows(b):
        for d in range(1, NX):
            x_copy(b, d).wait_recv()
        cs[...] = combine(combine(xs[b, 0], xr[b, 1]), combine(xr[b, 0], xr[b, 2]))
        c_copy.start()

    half = D // 2
    mine_at = pl.multiple_of(c * half, half)
    mine_cols = pl.ds(mine_at, half)
    a_cols = pl.ds(mine_at, half // 2)
    b_cols = pl.ds(pl.multiple_of(mine_at + half // 2, half // 2), half // 2)
    a0_cols = pl.ds(mine_at, half - SIDE)
    b0_cols = pl.ds(pl.multiple_of(mine_at + half - SIDE, 128), SIDE)
    far_order = (4, 3, 5, 2, 6, 1, 7)
    order = [3, 1, 2]
    neighbours = [at_x(1), at_x(3), at_y(1), at_y(3)]

    def same(view, send, recv, target):
        return remote(view, view, send, recv, target)

    def z_block(d, target):
        view = wbuf.at[y, (z + d) % NZ, x, :, mine_cols]
        return same(view, gzs_sem.at[target - 1], gzr_sem.at[target - 1], at_z(target))

    def block(ey, ex, cols):
        return wbuf.at[(y + ey) % NY, :, (x + ex) % NX, :, cols]

    def sib_copy(ey, ex, column_start):
        cols = pl.ds(pl.multiple_of(column_start, half), half)
        return same(block(ey, ex, cols), gss_sem.at[ey, ex], gsr_sem.at[ey, ex], sibling)

    def to_sibling(ey, ex):
        sib_copy(ey, ex, mine_at).start()

    def update_rows():
        mv_copy.wait()
        mine, other = own_mv[...], sib_mv[...]
        first = c == 0
        lower, upper = jnp.where(first, mine, other), jnp.where(first, other, mine)
        moments = [jnp.concatenate([lower[i], upper[i]], axis=0) for i in range(2)]
        old_rows = w_v[pl.ds(pl.multiple_of(me // 2 * 8, 8), 8), :]
        c_copy.wait()
        summed = combine(cs[...], cr[...])
        new_rows, new_first, new_second = adam_update(summed, old_rows, moments[0], moments[1])
        wbuf[y, z, x, :, mine_cols] = jnp.where(first, new_rows[:, :half], new_rows[:, half:])
        for d in far_order:
            z_block(0, d).start()
        return first, new_first, new_second

    def keep_moments(first, new_first, new_second):
        m_v[...] = jnp.where(first, new_first[:4], new_first[4:])
        v_v[...] = jnp.where(first, new_second[:4], new_second[4:])

    def x_column(d, ex):
        return same(block(0, ex, mine_cols), gxs_sem.at[d - 1], gxr_sem.at[d - 1], at_x(d))

    def y_column(k, e, ey, ex):
        i = 3 * k + e - 1
        cols = mine_cols if ex == 0 else a0_cols
        return same(block(ey, ex, cols), gys_sem.at[i], gyr_sem.at[i], at_y(e))

    def y_side(e, d, ex):
        i = 3 * (e - 1) + d - 1
        return same(block(NY - e, ex, b0_cols), y0s_sem.at[i], y0r_sem.at[i], at_x(d))

    def turn(i):
        at = slice(256 * i, 256 * i + 256)
        thp[:, at], tlp[:, at] = split(ttp[at, :].T)

    def following(b, pair, columns):
        for ey in (pair, pair + 2):
            for ex in columns:
                sib_copy(ey, ex, (1 - c) * half).wait_recv()
        p = (y + pair) % 2
        parts = [
            jnp.stack([wbuf[p + 2 * i, :, b], wbuf[p + 2 * i, :, b + 2]], axis=1).reshape(128, D)
            for i in range(2)
        ]
        lanes = pl.ds(pl.multiple_of((2 * b + p) * 256, 256), 256)
        wh, wl = split(jnp.concatenate(parts, axis=0))
        return dot3(thp[:, lanes], tlp[:, lanes], wh, wl, ((1,), (0,)))

    filler(NZ - 1)
    reduce_sends(0)
    for s in range(NZ - 1):
        y_step(1, s)
        if s in (1, 3, 5, 6):
            turn((1, 3, 5, 6).index(s))
        if s == 1:

            @pl.when(even)
            def _():
                gather_rows(0)

        if s == 2:

            @pl.when(even)
            def _():
                keep_moments(*update_rows())

        if s == 4:

            @pl.when(even)
            def _():
                for d in far_order:
                    z_block(NZ - d, d).wait_recv()
                for d in (2, 1, 3):
                    x_column(d, 0).start()
                to_sibling(0, 0)

    reduce_sends(1)

    def far_block(j, d):
        return wbuf.at[(y + 2) % NY, (z + d) % NZ, (x + NX - FAR[j]) % NX, :, mine_cols]

    def far_first(j):
        return same(far_block(j, 0), fis_sem.at[j], fir_sem.at[j], far(FAR[j]))

    def far_copy(j, at, d):
        i = j * (NZ - 1) + d - 1
        return same(far_block(j, at), fzs_sem.at[i], fzr_sem.at[i], at_z(d))

    def two_away(i, ey, ex):
        target = at_x(2) if i == 0 else at_y(2)
        return same(block(ey, ex, mine_cols), g2s_sem.at[i], g2r_sem.at[i], target)

    def from_neighbour(i):
        ey, ex = [(0, 3), (0, 1), (3, 0), (1, 0)][i]
        return same(block(ey, ex, mine_cols), gns_sem.at[i], gnr_sem.at[i], neighbours[i])

    def a_flow(k, direction, ey):
        i = 2 * k + direction
        return same(block(ey, order[k], a_cols), gas_sem.at[i], gar_sem.at[i], neighbours[2 + direction])

    def b_flow(k, target, ex):
        i = 3 * k + target
        return same(
            block(order[k], ex, b_cols), gbs_sem.at[i], gbr_sem.at[i], at_x((1, 3, 2)[target])
        )

    def y_column_out(k, ex):
        for e in (2, 1, 3):
            y_column(k, e, 0, ex).start()

    def y_column_in(k, ex, d):
        for e in (1, 3, 2):
            y_column(k, e, NY - e, ex).wait_recv()
            y_side(e, d, ex).wait_recv()
            to_sibling(NY - e, ex)

    def far_in(js):
        for j in js:
            far_first(j).wait_recv()
            for d in far_order:
                far_copy(j, 0, d).start()

    def far_columns_in(js):
        for j in js:
            for d in far_order:
                far_copy(j, NZ - d, d).wait_recv()
            to_sibling(2, NX - FAR[j])

    def drain(columns, own, js, as_, bs):
        for k, ex in enumerate(columns):
            for e in range(1, NY):
                y_column(k, e, 0, ex).wait_send()
        for d in range(1, NZ):
            z_block(0, d).wait_send()
            for j in js:
                far_copy(j, 0, d).wait_send()
        for k, direction in as_:
            a_flow(k, direction, 0).wait_send()
        for k, target in bs:
            b_flow(k, target, 0).wait_send()

    @pl.when(odd)
    def _():
        def to_neighbours(d):
            view = wbuf.at[y, (z + d) % NZ, x, :, mine_cols]
            for i, target in enumerate(neighbours):
                same(view, gns_sem.at[i], gnr_sem.at[i], target).start()
            same(view, g2s_sem.at[0], g2r_sem.at[0], at_x(2)).start()

        x_column(1, 3).wait_recv()
        x_column(3, 1).wait_recv()
        y_column_out(0, 3)
        y_column_out(1, 1)
        to_sibling(0, 3)
        to_sibling(0, 1)
        gather_rows(1)
        updated = update_rows()
        for i in range(3):
            same(wbuf.at[y, z, x, :, mine_cols], fis_sem.at[i], fir_sem.at[i], far(FAR[i])).start()
        to_neighbours(0)
        keep_moments(*updated)
        for d in (1, 7, 2, 6, 3, 5, 4):
            z_block(NZ - d, d).wait_recv()
            to_neighbours(NZ - d)
        two_away(1, 0, 0).start()
        far_in((0,))
        to_sibling(0, 0)
        for k in range(2):
            from_neighbour(2 + k).wait_recv()
            for target in (2, 0, 1):
                b_flow(k, target, 0).start()
            to_sibling(order[k], 0)
        two_away(0, 0, 2).wait_recv()
        for direction in range(2):
            a_flow(2, direction, 0).start()
        to_sibling(0, 2)
        y_column_in(0, 3, 1)
        y_column_in(1, 1, 3)
        two_away(1, 2, 0).wait_recv()
        to_sibling(2, 0)
        far_columns_in((0,))
        next_v[...] = following(0, 0, (3, 1))
        next_v[...] += following(0, 1, (3, 1))
        next_v[...] += following(1, 0, (0, 2))
        for direction in range(2):
            a_flow(2, direction, order[direction]).wait_recv()
            b_flow(direction, 2, 2).wait_recv()
            to_sibling(order[direction], 2)
        next_v[...] += following(1, 1, (0, 2))
        for i in range(3):
            same(wbuf.at[y, z, x, :, mine_cols], fis_sem.at[i], fir_sem.at[i], far(FAR[i])).wait_send()
        for i in range(4):
            from_neighbour(i).wait_send()
        for i in range(2):
            two_away(i, 0, 0).wait_send()
        for d in (1, 3):
            x_copy(0, d).wait_send()
        x_copy(1, 2).wait_send()
        drain(
            (3, 1), True, (0,), [(2, 0), (2, 1)], [(k, t) for k in range(2) for t in range(3)]
        )

    @pl.when(even)
    def _():
        x_column(2, 2).wait_recv()
        y_column_out(0, 0)
        y_column_out(1, 2)
        to_sibling(0, 2)
        for e in (1, 3, 2):
            y_column(0, e, NY - e, 0).wait_recv()
            for d in (2, 1, 3):
                y_side(e, d, 0).start()
            to_sibling(NY - e, 0)
        far_in((1, 2))
        for k in range(2):
            from_neighbour(k).wait_recv()
            for direction in range(2):
                a_flow(k, direction, 0).start()
            to_sibling(0, order[k])
        y_column_in(1, 2, 2)
        far_columns_in((1, 2))
        next_v[...] = following(0, 0, (0, 2))
        next_v[...] += following(0, 1, (0, 2))
        next_v[...] += following(1, 0, (3, 1))
        for k in range(2):
            for direction in range(2):
                a_flow(k, direction, order[direction]).wait_recv()
                b_flow(direction, k, order[k]).wait_recv()
                to_sibling(order[direction], order[k])
        next_v[...] += following(1, 1, (3, 1))
        for d in range(1, NX):
            x_column(d, 0).wait_send()
            for e in range(1, NY):
                y_side(e, d, 0).wait_send()
        for d in (1, 3):
            x_copy(1, d).wait_send()
        x_copy(0, 2).wait_send()
        drain((0, 2), False, (1, 2), [(k, i) for k in range(2) for i in range(2)], [])

    def y_drain(s, carry):
        for b in range(2):
            for d in range(1, NY):
                y_copy(b, s, d).wait_send()
        return carry

    lax.fori_loop(0, NZ, y_drain, 0)
    for b in range(2):
        for d in range(1, NZ):
            z_copy(b, 0, d).wait_send()
    for ey in range(NY):
        for ex in range(NX):
            sib_copy(ey, ex, mine_at).wait_send()


PIECES = (2, 2, 2, 4, 1, 1)


def store_kernel(*refs):
    sources, targets, sem = refs[:6], refs[6:12], refs[12]
    copies = []
    for i, (source, target) in enumerate(zip(sources, targets)):
        count = PIECES[i]
        size = source.shape[0] // count
        for j in range(count):
            rows = pl.ds(j * size, size)
            copies.append(pltpu.make_async_copy(source.at[rows], target.at[rows], sem.at[len(copies)]))
    for copy in copies:
        copy.start()
    for copy in copies:
        copy.wait()


def on_device(tokens, cotangent, weight, first_moment, second_moment):
    dma = pltpu.SemaphoreType.DMA
    any_space = pl.BlockSpec(memory_space=pl.ANY)
    rows = lambda *shape: pltpu.VMEM(shape + (D,), F32)
    shapes = [(T, D), (T, D), (T, D), (NY, NZ, NX, 8, D), (4, D), (4, D)]
    held = pl.pallas_call(
        exchange_kernel,
        out_shape=[pltpu.VMEM(shape, F32) for shape in shapes],
        in_specs=[any_space] * 5,
        out_specs=[pl.BlockSpec(memory_space=pltpu.VMEM)] * 6,
        scratch_shapes=[
            rows(T), rows(T), rows(D),
            pltpu.VMEM((D, T), BF16), pltpu.VMEM((D, T), BF16), pltpu.VMEM((D, T), F32),
            pltpu.VMEM((T, D), BF16), pltpu.VMEM((T, D), BF16),
            pltpu.VMEM((T, D), BF16), pltpu.VMEM((T, D), BF16),
            pltpu.VMEM((T, D), BF16), pltpu.VMEM((T, D), BF16),
            rows(NZ, NY, NX, 8), rows(NY - 1, NZ, NX, 8),
            rows(NZ, NX, 8), rows(NZ - 1, NX, 8), rows(2, 2, 2, 8),
            rows(2, NX, 8), rows(2, NX - 1, 8), rows(8), rows(8),
            rows(2, 4), rows(2, 4),
            dma((5,)),
            dma((2, NY - 1, NZ)), dma((2, NY - 1, NZ)), dma((2, NZ - 1)), dma((2, NZ - 1)),
            dma((2, NX - 1)), dma((2, NX - 1)), dma((2,)), dma((2,)),
            dma((NZ - 1,)), dma((NZ - 1,)), dma((NX - 1,)), dma((NX - 1,)),
            dma((6,)), dma((6,)), dma((4,)), dma((4,)), dma((2,)), dma((2,)),
            dma((9,)), dma((9,)), dma((3,)), dma((3,)), dma((3 * (NZ - 1),)), dma((3 * (NZ - 1),)),
            dma((6,)), dma((6,)), dma((6,)), dma((6,)),
            dma((NY, NX)), dma((NY, NX)),
        ],
        compiler_params=pltpu.CompilerParams(
            collective_id=0, has_side_effects=True, vmem_limit_bytes=52 * 2**20
        ),
        name="exchange",
    )(tokens, cotangent, weight, first_moment, second_moment)
    projected, input_grad, next_projected, new_weight, new_first, new_second = pl.pallas_call(
        store_kernel,
        out_shape=[jax.ShapeDtypeStruct(shape, F32) for shape in shapes],
        in_specs=[any_space] * 6,
        out_specs=[pl.BlockSpec(memory_space=pltpu.HBM)] * 6,
        scratch_shapes=[dma((sum(PIECES),))],
        compiler_params=pltpu.CompilerParams(vmem_limit_bytes=2**20),
        name="store",
    )(*held)
    new_weight = new_weight.reshape(D, D)
    return (projected, input_grad, new_weight, new_first, new_second, next_projected)


def solution(mesh):
    placed = (P("dp", None), P("dp", None), P(), P("dp", None), P("dp", None))
    return jax.shard_map(
        on_device,
        mesh=mesh,
        in_specs=placed,
        out_specs=(P("dp", None), P("dp", None), P(), P("dp", None), P("dp", None), P("dp", None)),
        check_vma=False,
    )
```

```python
import jax
import jax.numpy as jnp
from jax import lax
from jax.experimental import pallas as pl
from jax.experimental.pallas import tpu as pltpu
from jax.sharding import PartitionSpec as P

beta_one = 0.9
beta_two = 0.999
rate_value = 0.01
step_count = 10
adam_epsilon = 1e-08
norm_epsilon = 1e-06

MESH = pl.DeviceIdType.MESH
NY, NZ, NX = 4, 8, 4
D = 1024
T = 256
CH = D // (NY * NZ)
FAR = (2, 1, 3)
SIDE = 256
F32, BF16 = jnp.float32, jnp.bfloat16


def combine(left_rows, right_rows):
    cross_term = jnp.sum(left_rows * right_rows, axis=-1, keepdims=True)
    left_norm = jnp.sum(left_rows * left_rows, axis=-1, keepdims=True)
    right_norm = jnp.sum(right_rows * right_rows, axis=-1, keepdims=True)
    left_coef = 1.0 - cross_term / (2.0 * (left_norm + norm_epsilon))
    right_coef = 1.0 - cross_term / (2.0 * (right_norm + norm_epsilon))
    return left_coef * left_rows + right_coef * right_rows


def adam_update(gradient, weight_rows, first_rows, second_rows):
    first_new = beta_one * first_rows + (1.0 - beta_one) * gradient
    second_new = beta_two * second_rows + (1.0 - beta_two) * gradient * gradient
    first_hat = first_new / (1.0 - beta_one**step_count)
    second_hat = second_new / (1.0 - beta_two**step_count)
    weight_new = weight_rows - rate_value * first_hat / (jnp.sqrt(second_hat) + adam_epsilon)
    return (weight_new, first_new, second_new)


def split(value):
    high = value.astype(BF16)
    return high, (value - high.astype(F32)).astype(BF16)


def dot(a, b, contract):
    return lax.dot_general(a, b, (contract, ((), ())), preferred_element_type=F32)


def dot3(a_high, a_low, b_high, b_low, contract):
    return (
        dot(a_high, b_high, contract)
        + dot(a_high, b_low, contract)
        + dot(a_low, b_high, contract)
    )


def offset_of(s):
    return 4 + (s + 1) // 2 * (1 - 2 * (s % 2))


def exchange_kernel(
    tok_hbm, cot_hbm, w_hbm, m_hbm, v_hbm,
    proj_v, igrad_v, next_v, wbuf, m_v, v_v,
    tok_v, cot_v, w_v, tth, ttl, ttp, th, tl, thp, tlp, ch, cl,
    g, yr, zs, zr, zz, xs, xr, cs, cr, own_mv, sib_mv,
    in_sem, yhs_sem, yhr_sem, zhs_sem, zhr_sem, ys_sem, yr_sem, zs_sem, zr_sem, xs_sem, xr_sem, cs_sem, cr_sem,
    gzs_sem, gzr_sem, gxs_sem, gxr_sem, gys_sem, gyr_sem, gns_sem, gnr_sem, g2s_sem, g2r_sem,
    y0s_sem, y0r_sem, fis_sem, fir_sem, fzs_sem, fzr_sem, gas_sem, gar_sem, gbs_sem, gbr_sem, gss_sem, gsr_sem,
):
    me = lax.axis_index("dp")
    c = me % 2
    x = me // 2 % NX
    z = me // (2 * NX) % NZ
    y = me // (2 * NX * NZ)
    odd = x % 2 == 1
    even = x % 2 == 0
    owns = [even, odd]
    others = [odd, even]

    def device(yy, zz, xx, cc):
        return (((yy * NZ + zz) * NX + xx) * 2 + cc,)

    def at_y(d):
        return device((y + d) % NY, z, x, c)

    def at_z(d):
        return device(y, (z + d) % NZ, x, c)

    def at_x(d):
        return device(y, z, (x + d) % NX, c)

    sibling = device(y, z, x, 1 - c)

    def far(ex):
        return device((y + 2) % NY, z, (x + ex) % NX, c)

    def remote(src, dst, send, recv, target):
        return pltpu.make_async_remote_copy(
            src_ref=src, dst_ref=dst, send_sem=send, recv_sem=recv,
            device_id=target, device_id_type=MESH,
        )

    quarters = [pl.ds(256 * i, 256) for i in range(4)]
    pairs = [(tok_hbm.at[:, at], tok_v.at[:, at]) for at in quarters]
    pairs += [(cot_hbm.at[:, at], cot_v.at[:, at]) for at in quarters]
    pairs += [(m_hbm, own_mv.at[0]), (v_hbm, own_mv.at[1]), (w_hbm, w_v)]
    loads = [pltpu.make_async_copy(src, dst, in_sem.at[i]) for i, (src, dst) in enumerate(pairs)]
    for load in loads[:10]:
        load.start()

    barrier = pltpu.get_barrier_semaphore()
    partners = (
        [at_y(d) for d in range(1, NY)]
        + [at_z(d) for d in range(1, NZ)]
        + [at_x(d) for d in range(1, NX)]
        + [far(ex) for ex in FAR]
        + [sibling]
    )
    for partner in partners:
        pl.semaphore_signal(barrier, inc=1, device_id=partner, device_id_type=MESH)

    for j in range(D // 128):
        lanes = slice(128 * j, 128 * j + 128)
        if j % 2 == 0:
            loads[j // 2].wait()
        tth[lanes, :], ttl[lanes, :] = split(tok_v[:, lanes].T * (1.0 / T))
    for j in range(D // 256):
        lanes = slice(256 * j, 256 * j + 256)
        loads[4 + j].wait()
        ch[:, lanes], cl[:, lanes] = split(cot_v[:, lanes])
    loads[8].wait()
    loads[9].wait()
    loads[10].start()
    pl.semaphore_wait(barrier, len(partners))

    mv_copy = remote(own_mv, sib_mv, cs_sem.at[1], cr_sem.at[1], sibling)
    mv_copy.start()

    def y_copy(b, s, d):
        rows = pl.ds(2 * b, 2)
        return remote(
            g.at[s, d, rows], yr.at[d - 1, s, rows],
            ys_sem.at[b, d - 1, s], yr_sem.at[b, d - 1, s], at_y(d),
        )

    def y_half(i, d):
        rows = pl.ds(2 + i, 1)
        return remote(
            g.at[NZ - 2, d, rows], yr.at[d - 1, NZ - 2, rows],
            yhs_sem.at[i, d - 1], yhr_sem.at[i, d - 1], at_y(d),
        )

    def z_half(i):
        rows = pl.ds(2 + i, 1)
        return remote(
            zs.at[NZ - 2, rows], zr.at[NZ - 2, rows], zhs_sem.at[i], zhr_sem.at[i], at_z(NZ - 1)
        )

    def z_copy(b, s, d):
        rows = pl.ds(2 * b, 2)
        return remote(
            zs.at[s, rows], zr.at[d - 1, rows], zs_sem.at[b, d - 1], zr_sem.at[b, d - 1], at_z(d)
        )

    def gradient_step(s, carry):
        owner = (z + offset_of(s)) % NZ
        starts = [
            pl.multiple_of((y + d) % NY * (D // NY) + owner * CH, CH) for d in range(NY)
        ]
        high = [tth[pl.ds(start, CH), :] for start in starts]
        low = [ttl[pl.ds(start, CH), :] for start in starts]
        count = NY * CH
        both = dot(jnp.concatenate(high + low, axis=0), ch[...], ((1,), (0,)))
        rest = dot(jnp.concatenate(high, axis=0), cl[...], ((1,), (0,)))
        value = both[:count] + both[count:] + rest
        for d in range(NY):
            for i in range(NX):
                at = d * CH + 8 * i
                g[s, d, 2 * (i % 2) + i // 2] = value[at : at + 8]
        for d in (2, 1, 3):
            y_copy(0, s, d).start()
        return carry

    lax.fori_loop(0, NZ, gradient_step, 0)

    def second_sends(s, carry):
        for d in (2, 1, 3):
            y_copy(1, s, d).start()
        return carry

    lax.fori_loop(0, NZ - 2, second_sends, 0)
    for i in range(2):
        for d in (2, 1, 3):
            y_half(i, d).start()
    second_sends(NZ - 1, 0)

    for j in range(D // 128):
        lanes = slice(128 * j, 128 * j + 128)
        piece = tok_v[:, lanes]
        th[:, lanes], tl[:, lanes] = split(piece)
        turned = piece.T.reshape(4, NX, 8, T)
        plane, quarter = j // 2, j % 2
        for b in range(2):
            at = (2 * b + plane % 2) * 256 + plane // 2 * 128 + quarter * 64
            ttp[at : at + 64] = jnp.stack([turned[:, b], turned[:, b + 2]], axis=1).reshape(64, T)
    loads[10].wait()

    def y_step(b, s):
        for d in range(1, NY):
            y_copy(b, s, d).wait_recv()
        rows = pl.ds(2 * b, 2)
        across = combine(g[s, 0, rows], yr[1, s, rows])
        zs[s, rows] = combine(across, combine(yr[0, s, rows], yr[2, s, rows]))
        z_copy(b, s, offset_of(s)).start()

    def y_step_halves():
        s = NZ - 2
        for i in range(2):
            for d in range(1, NY):
                y_half(i, d).wait_recv()
            q = 2 + i
            across = combine(g[s, 0, q], yr[1, s, q])
            zs[s, q] = combine(across, combine(yr[0, s, q], yr[2, s, q]))
            z_half(i).start()

    def filler(s):
        @pl.when(s < 4)
        def _():
            lanes = pl.ds(pl.multiple_of(s * 256, 256), 256)
            wh, wl = split(w_v[:, lanes])
            proj_v[:, lanes] = dot3(th[...], tl[...], wh, wl, ((1,), (0,)))

        @pl.when(s >= 4)
        def _():
            lanes = pl.ds(pl.multiple_of((s - 4) * 256, 256), 256)
            wh, wl = split(w_v[lanes, :])
            igrad_v[:, lanes] = dot3(ch[...], cl[...], wh, wl, ((1,), (1,)))

    def first_step(s, carry):
        y_step(0, s)
        filler(s)
        return carry

    lax.fori_loop(0, NZ - 1, first_step, 0)

    def z_pair(b, d):
        for at in (d, d + 4):
            z_copy(b, 0, at).wait_recv()
        rows = pl.ds(2 * b, 2)
        return combine(zr[d - 1, rows], zr[d + 3, rows])

    def x_copy(b, d):
        return remote(
            xs.at[b, d], xr.at[b, d - 1], xs_sem.at[b, d - 1], xr_sem.at[b, d - 1], at_x(d)
        )

    def reduce_sends(b):
        zz[b, 0] = z_pair(b, 2)
        zz[b, 1] = z_pair(b, 1)
        for d in (3, 4):
            z_copy(b, 0, d).wait_recv()
        if b == 0:
            z_copy(b, 0, 7).wait_recv()
        last = NZ - 1
        for d in range(1, NY):
            y_copy(b, last, d).wait_recv()

        def early(d):
            h = (x + d) % NX // 2
            q = 2 * b + h
            across = combine(g[last, 0, q], yr[1, last, q])
            across = combine(across, combine(yr[0, last, q], yr[2, last, q]))
            xs[b, d] = combine(combine(across, zr[3, q]), zz[b, 0, h])

        def late(d):
            h = (x + d) % NX // 2
            q = 2 * b + h
            if b == 1:
                z_half(h).wait_recv()
            rest = combine(zz[b, 1, h], combine(zr[2, q], zr[6, q]))
            xs[b, d] = combine(xs[b, d], rest)

        @pl.when(owns[b])
        def _():
            early(2)
            early(0)
            late(2)
            x_copy(b, 2).start()
            late(0)

        @pl.when(others[b])
        def _():
            early(1)
            early(3)
            for d in (1, 3):
                late(d)
                x_copy(b, d).start()

    c_copy = remote(cs, cr, cs_sem.at[0], cr_sem.at[0], sibling)

    def gather_rows(b):
        for d in range(1, NX):
            x_copy(b, d).wait_recv()
        cs[...] = combine(combine(xs[b, 0], xr[b, 1]), combine(xr[b, 0], xr[b, 2]))
        c_copy.start()

    half = D // 2
    mine_at = pl.multiple_of(c * half, half)
    mine_cols = pl.ds(mine_at, half)
    a_cols = pl.ds(mine_at, half // 2)
    b_cols = pl.ds(pl.multiple_of(mine_at + half // 2, half // 2), half // 2)
    a0_cols = pl.ds(mine_at, half - SIDE)
    b0_cols = pl.ds(pl.multiple_of(mine_at + half - SIDE, 128), SIDE)
    far_order = (4, 3, 5, 2, 6, 1, 7)
    order = [3, 1, 2]
    neighbours = [at_x(1), at_x(3), at_y(1), at_y(3)]

    def same(view, send, recv, target):
        return remote(view, view, send, recv, target)

    def z_block(d, target):
        view = wbuf.at[y, (z + d) % NZ, x, :, mine_cols]
        return same(view, gzs_sem.at[target - 1], gzr_sem.at[target - 1], at_z(target))

    def block(ey, ex, cols):
        return wbuf.at[(y + ey) % NY, :, (x + ex) % NX, :, cols]

    def sib_copy(ey, ex, column_start):
        cols = pl.ds(pl.multiple_of(column_start, half), half)
        return same(block(ey, ex, cols), gss_sem.at[ey, ex], gsr_sem.at[ey, ex], sibling)

    def to_sibling(ey, ex):
        sib_copy(ey, ex, mine_at).start()

    def update_rows():
        mv_copy.wait()
        mine, other = own_mv[...], sib_mv[...]
        first = c == 0
        lower, upper = jnp.where(first, mine, other), jnp.where(first, other, mine)
        moments = [jnp.concatenate([lower[i], upper[i]], axis=0) for i in range(2)]
        old_rows = w_v[pl.ds(pl.multiple_of(me // 2 * 8, 8), 8), :]
        c_copy.wait()
        summed = combine(cs[...], cr[...])
        new_rows, new_first, new_second = adam_update(summed, old_rows, moments[0], moments[1])
        wbuf[y, z, x, :, mine_cols] = jnp.where(first, new_rows[:, :half], new_rows[:, half:])
        for d in far_order:
            z_block(0, d).start()
        return first, new_first, new_second

    def keep_moments(first, new_first, new_second):
        m_v[...] = jnp.where(first, new_first[:4], new_first[4:])
        v_v[...] = jnp.where(first, new_second[:4], new_second[4:])

    def x_column(d, ex):
        return same(block(0, ex, mine_cols), gxs_sem.at[d - 1], gxr_sem.at[d - 1], at_x(d))

    def y_column(k, e, ey, ex):
        i = 3 * k + e - 1
        cols = mine_cols if ex % 2 == 0 else a0_cols
        return same(block(ey, ex, cols), gys_sem.at[i], gyr_sem.at[i], at_y(e))

    def y_side(e, d, ex):
        i = 3 * (e - 1) + d - 1
        return same(block(NY - e, ex, b0_cols), y0s_sem.at[i], y0r_sem.at[i], at_x(d))

    def turn(i):
        at = slice(256 * i, 256 * i + 256)
        thp[:, at], tlp[:, at] = split(ttp[at, :].T)

    def following(b, pair, columns):
        for ey in (pair, pair + 2):
            for ex in columns:
                sib_copy(ey, ex, (1 - c) * half).wait_recv()
        p = (y + pair) % 2
        parts = [
            jnp.stack([wbuf[p + 2 * i, :, b], wbuf[p + 2 * i, :, b + 2]], axis=1).reshape(128, D)
            for i in range(2)
        ]
        lanes = pl.ds(pl.multiple_of((2 * b + p) * 256, 256), 256)
        wh, wl = split(jnp.concatenate(parts, axis=0))
        return dot3(thp[:, lanes], tlp[:, lanes], wh, wl, ((1,), (0,)))

    filler(NZ - 1)
    reduce_sends(0)
    for s in range(NZ - 1):
        if s < NZ - 2:
            y_step(1, s)
        else:
            y_step_halves()
        if s in (1, 3, 5, 6):
            turn((1, 3, 5, 6).index(s))
        if s == 1:

            @pl.when(even)
            def _():
                gather_rows(0)

        if s == 2:

            @pl.when(even)
            def _():
                keep_moments(*update_rows())

        if s == 4:

            @pl.when(even)
            def _():
                for d in far_order:
                    z_block(NZ - d, d).wait_recv()
                for d in (2, 1, 3):
                    x_column(d, 0).start()
                to_sibling(0, 0)

    reduce_sends(1)

    def far_block(j, d):
        return wbuf.at[(y + 2) % NY, (z + d) % NZ, (x + NX - FAR[j]) % NX, :, mine_cols]

    def far_first(j):
        return same(far_block(j, 0), fis_sem.at[j], fir_sem.at[j], far(FAR[j]))

    def far_copy(j, at, d):
        i = j * (NZ - 1) + d - 1
        return same(far_block(j, at), fzs_sem.at[i], fzr_sem.at[i], at_z(d))

    def two_away(i, ey, ex):
        target = at_x(2) if i == 0 else at_y(2)
        return same(block(ey, ex, mine_cols), g2s_sem.at[i], g2r_sem.at[i], target)

    def from_neighbour(i):
        ey, ex = [(0, 3), (0, 1), (3, 0), (1, 0)][i]
        return same(block(ey, ex, mine_cols), gns_sem.at[i], gnr_sem.at[i], neighbours[i])

    def a_flow(k, direction, ey):
        i = 2 * k + direction
        return same(block(ey, order[k], a_cols), gas_sem.at[i], gar_sem.at[i], neighbours[2 + direction])

    def b_flow(k, target, ex):
        i = 3 * k + target
        return same(
            block(order[k], ex, b_cols), gbs_sem.at[i], gbr_sem.at[i], at_x((1, 3, 2)[target])
        )

    def y_column_out(k, ex):
        for e in (2, 1, 3):
            y_column(k, e, 0, ex).start()

    def y_column_in(k, ex, d):
        for e in (1, 3, 2):
            y_column(k, e, NY - e, ex).wait_recv()
            if d != 2:
                y_side(e, d, ex).wait_recv()
            to_sibling(NY - e, ex)

    def far_in(js):
        for j in js:
            far_first(j).wait_recv()
            for d in far_order:
                far_copy(j, 0, d).start()

    def far_columns_in(js):
        for j in js:
            for d in far_order:
                far_copy(j, NZ - d, d).wait_recv()
            to_sibling(2, NX - FAR[j])

    def drain(columns, own, js, as_, bs):
        for k, ex in enumerate(columns):
            for e in range(1, NY):
                y_column(k, e, 0, ex).wait_send()
        for d in range(1, NZ):
            z_block(0, d).wait_send()
            for j in js:
                far_copy(j, 0, d).wait_send()
        for k, direction in as_:
            a_flow(k, direction, 0).wait_send()
        for k, target in bs:
            b_flow(k, target, 0).wait_send()

    @pl.when(odd)
    def _():
        def to_neighbours(d):
            view = wbuf.at[y, (z + d) % NZ, x, :, mine_cols]
            for i, target in enumerate(neighbours):
                same(view, gns_sem.at[i], gnr_sem.at[i], target).start()
            same(view, g2s_sem.at[0], g2r_sem.at[0], at_x(2)).start()

        x_column(1, 3).wait_recv()
        x_column(3, 1).wait_recv()
        y_column_out(0, 3)
        y_column_out(1, 1)
        to_sibling(0, 3)
        to_sibling(0, 1)
        gather_rows(1)
        updated = update_rows()
        for i in range(3):
            same(wbuf.at[y, z, x, :, mine_cols], fis_sem.at[i], fir_sem.at[i], far(FAR[i])).start()
        to_neighbours(0)
        keep_moments(*updated)
        for d in (1, 7, 2, 6, 3, 5, 4):
            z_block(NZ - d, d).wait_recv()
            to_neighbours(NZ - d)
        two_away(1, 0, 0).start()
        far_in((0,))
        to_sibling(0, 0)
        for k in range(2):
            from_neighbour(2 + k).wait_recv()
            for target in (2, 0, 1):
                b_flow(k, target, 0).start()
            to_sibling(order[k], 0)
        two_away(0, 0, 2).wait_recv()
        for direction in range(2):
            a_flow(2, direction, 0).start()
        to_sibling(0, 2)
        y_column_in(0, 3, 1)
        y_column_in(1, 1, 3)
        two_away(1, 2, 0).wait_recv()
        to_sibling(2, 0)
        far_columns_in((0,))
        next_v[...] = following(0, 0, (3, 1))
        next_v[...] += following(0, 1, (3, 1))
        next_v[...] += following(1, 0, (0, 2))
        for direction in range(2):
            a_flow(2, direction, order[direction]).wait_recv()
            b_flow(direction, 2, 2).wait_recv()
            to_sibling(order[direction], 2)
        next_v[...] += following(1, 1, (0, 2))
        for i in range(3):
            same(wbuf.at[y, z, x, :, mine_cols], fis_sem.at[i], fir_sem.at[i], far(FAR[i])).wait_send()
        for i in range(4):
            from_neighbour(i).wait_send()
        for i in range(2):
            two_away(i, 0, 0).wait_send()
        for d in (1, 3):
            x_copy(0, d).wait_send()
        x_copy(1, 2).wait_send()
        drain(
            (3, 1), True, (0,), [(2, 0), (2, 1)], [(k, t) for k in range(2) for t in range(3)]
        )

    @pl.when(even)
    def _():
        x_column(2, 2).wait_recv()
        y_column_out(0, 0)
        y_column_out(1, 2)
        to_sibling(0, 2)
        for e in (1, 3, 2):
            y_column(0, e, NY - e, 0).wait_recv()
            for d in (1, 3):
                y_side(e, d, 0).start()
            to_sibling(NY - e, 0)
        far_in((1, 2))
        for k in range(2):
            from_neighbour(k).wait_recv()
            for direction in range(2):
                a_flow(k, direction, 0).start()
            to_sibling(0, order[k])
        y_column_in(1, 2, 2)
        far_columns_in((1, 2))
        next_v[...] = following(0, 0, (0, 2))
        next_v[...] += following(0, 1, (0, 2))
        next_v[...] += following(1, 0, (3, 1))
        for k in range(2):
            for direction in range(2):
                a_flow(k, direction, order[direction]).wait_recv()
                b_flow(direction, k, order[k]).wait_recv()
                to_sibling(order[direction], order[k])
        next_v[...] += following(1, 1, (3, 1))
        for d in range(1, NX):
            x_column(d, 0).wait_send()
            if d != 2:
                for e in range(1, NY):
                    y_side(e, d, 0).wait_send()
        for d in (1, 3):
            x_copy(1, d).wait_send()
        x_copy(0, 2).wait_send()
        drain((0, 2), False, (1, 2), [(k, i) for k in range(2) for i in range(2)], [])

    def y_drain(s, carry):
        for d in range(1, NY):
            y_copy(0, s, d).wait_send()

        @pl.when(s != NZ - 2)
        def _():
            for d in range(1, NY):
                y_copy(1, s, d).wait_send()

        return carry

    lax.fori_loop(0, NZ, y_drain, 0)
    for i in range(2):
        for d in range(1, NY):
            y_half(i, d).wait_send()
        z_half(i).wait_send()
    for d in range(1, NZ):
        z_copy(0, 0, d).wait_send()
    for d in range(1, NZ - 1):
        z_copy(1, 0, d).wait_send()
    for ey in range(NY):
        for ex in range(NX):
            sib_copy(ey, ex, mine_at).wait_send()


PIECES = (2, 2, 2, 4, 1, 1)


def store_kernel(*refs):
    sources, targets, sem = refs[:6], refs[6:12], refs[12]
    copies = []
    for i, (source, target) in enumerate(zip(sources, targets)):
        count = PIECES[i]
        size = source.shape[0] // count
        for j in range(count):
            rows = pl.ds(j * size, size)
            copies.append(pltpu.make_async_copy(source.at[rows], target.at[rows], sem.at[len(copies)]))
    for copy in copies:
        copy.start()
    for copy in copies:
        copy.wait()


def on_device(tokens, cotangent, weight, first_moment, second_moment):
    dma = pltpu.SemaphoreType.DMA
    any_space = pl.BlockSpec(memory_space=pl.ANY)
    rows = lambda *shape: pltpu.VMEM(shape + (D,), F32)
    shapes = [(T, D), (T, D), (T, D), (NY, NZ, NX, 8, D), (4, D), (4, D)]
    held = pl.pallas_call(
        exchange_kernel,
        out_shape=[pltpu.VMEM(shape, F32) for shape in shapes],
        in_specs=[any_space] * 5,
        out_specs=[pl.BlockSpec(memory_space=pltpu.VMEM)] * 6,
        scratch_shapes=[
            rows(T), rows(T), rows(D),
            pltpu.VMEM((D, T), BF16), pltpu.VMEM((D, T), BF16), pltpu.VMEM((D, T), F32),
            pltpu.VMEM((T, D), BF16), pltpu.VMEM((T, D), BF16),
            pltpu.VMEM((T, D), BF16), pltpu.VMEM((T, D), BF16),
            pltpu.VMEM((T, D), BF16), pltpu.VMEM((T, D), BF16),
            rows(NZ, NY, NX, 8), rows(NY - 1, NZ, NX, 8),
            rows(NZ, NX, 8), rows(NZ - 1, NX, 8), rows(2, 2, 2, 8),
            rows(2, NX, 8), rows(2, NX - 1, 8), rows(8), rows(8),
            rows(2, 4), rows(2, 4),
            dma((11,)), dma((2, NY - 1)), dma((2, NY - 1)), dma((2,)), dma((2,)),
            dma((2, NY - 1, NZ)), dma((2, NY - 1, NZ)), dma((2, NZ - 1)), dma((2, NZ - 1)),
            dma((2, NX - 1)), dma((2, NX - 1)), dma((2,)), dma((2,)),
            dma((NZ - 1,)), dma((NZ - 1,)), dma((NX - 1,)), dma((NX - 1,)),
            dma((6,)), dma((6,)), dma((4,)), dma((4,)), dma((2,)), dma((2,)),
            dma((9,)), dma((9,)), dma((3,)), dma((3,)), dma((3 * (NZ - 1),)), dma((3 * (NZ - 1),)),
            dma((6,)), dma((6,)), dma((6,)), dma((6,)),
            dma((NY, NX)), dma((NY, NX)),
        ],
        compiler_params=pltpu.CompilerParams(
            collective_id=0, has_side_effects=True, vmem_limit_bytes=52 * 2**20
        ),
        name="exchange",
    )(tokens, cotangent, weight, first_moment, second_moment)
    projected, input_grad, next_projected, new_weight, new_first, new_second = pl.pallas_call(
        store_kernel,
        out_shape=[jax.ShapeDtypeStruct(shape, F32) for shape in shapes],
        in_specs=[any_space] * 6,
        out_specs=[pl.BlockSpec(memory_space=pltpu.HBM)] * 6,
        scratch_shapes=[dma((sum(PIECES),))],
        compiler_params=pltpu.CompilerParams(vmem_limit_bytes=2**20),
        name="store",
    )(*held)
    new_weight = new_weight.reshape(D, D)
    return (projected, input_grad, new_weight, new_first, new_second, next_projected)


def solution(mesh):
    placed = (P("dp", None), P("dp", None), P(), P("dp", None), P("dp", None))
    return jax.shard_map(
        on_device,
        mesh=mesh,
        in_specs=placed,
        out_specs=(P("dp", None), P("dp", None), P(), P("dp", None), P("dp", None), P("dp", None)),
        check_vma=False,
    )
```

```python
import jax
import jax.numpy as jnp
from jax import lax
from jax.experimental import pallas as pl
from jax.experimental.pallas import tpu as pltpu
from jax.sharding import PartitionSpec as P

beta_one = 0.9
beta_two = 0.999
rate_value = 0.01
step_count = 10
adam_epsilon = 1e-08
norm_epsilon = 1e-06

MESH = pl.DeviceIdType.MESH
NY, NZ, NX = 4, 8, 4
D = 1024
T = 256
CH = D // (NY * NZ)
FAR = (2, 1, 3)
SIDE = 256
F32, BF16 = jnp.float32, jnp.bfloat16


def combine(left_rows, right_rows):
    cross_term = jnp.sum(left_rows * right_rows, axis=-1, keepdims=True)
    left_norm = jnp.sum(left_rows * left_rows, axis=-1, keepdims=True)
    right_norm = jnp.sum(right_rows * right_rows, axis=-1, keepdims=True)
    left_coef = 1.0 - cross_term / (2.0 * (left_norm + norm_epsilon))
    right_coef = 1.0 - cross_term / (2.0 * (right_norm + norm_epsilon))
    return left_coef * left_rows + right_coef * right_rows


def adam_update(gradient, weight_rows, first_rows, second_rows):
    first_new = beta_one * first_rows + (1.0 - beta_one) * gradient
    second_new = beta_two * second_rows + (1.0 - beta_two) * gradient * gradient
    first_hat = first_new / (1.0 - beta_one**step_count)
    second_hat = second_new / (1.0 - beta_two**step_count)
    weight_new = weight_rows - rate_value * first_hat / (jnp.sqrt(second_hat) + adam_epsilon)
    return (weight_new, first_new, second_new)


def split(value):
    high = value.astype(BF16)
    return high, (value - high.astype(F32)).astype(BF16)


def dot(a, b, contract):
    return lax.dot_general(a, b, (contract, ((), ())), preferred_element_type=F32)


def dot3(a_high, a_low, b_high, b_low, contract):
    return (
        dot(a_high, b_high, contract)
        + dot(a_high, b_low, contract)
        + dot(a_low, b_high, contract)
    )


def offset_of(s):
    return 4 + (s + 1) // 2 * (1 - 2 * (s % 2))


def exchange_kernel(
    tok_hbm, cot_hbm, w_hbm, m_hbm, v_hbm,
    proj_v, igrad_v, next_v, wbuf, m_v, v_v,
    tok_v, cot_v, w_v, tth, ttl, ttp, th, tl, thp, tlp, ch, cl,
    g, yr, zs, zr, zz, xs, xr, cs, cr, own_mv, sib_mv,
    in_sem, yhs_sem, yhr_sem, zhs_sem, zhr_sem, ys_sem, yr_sem, zs_sem, zr_sem, xs_sem, xr_sem, cs_sem, cr_sem,
    gzs_sem, gzr_sem, gxs_sem, gxr_sem, gys_sem, gyr_sem, gns_sem, gnr_sem, g2s_sem, g2r_sem,
    y0s_sem, y0r_sem, fis_sem, fir_sem, fzs_sem, fzr_sem, gas_sem, gar_sem, gbs_sem, gbr_sem, gss_sem, gsr_sem,
):
    me = lax.axis_index("dp")
    c = me % 2
    x = me // 2 % NX
    z = me // (2 * NX) % NZ
    y = me // (2 * NX * NZ)
    odd = x % 2 == 1
    even = x % 2 == 0
    owns = [even, odd]
    others = [odd, even]

    def device(yy, zz, xx, cc):
        return (((yy * NZ + zz) * NX + xx) * 2 + cc,)

    def at_y(d):
        return device((y + d) % NY, z, x, c)

    def at_z(d):
        return device(y, (z + d) % NZ, x, c)

    def at_x(d):
        return device(y, z, (x + d) % NX, c)

    sibling = device(y, z, x, 1 - c)

    def far(ex):
        return device((y + 2) % NY, z, (x + ex) % NX, c)

    def remote(src, dst, send, recv, target):
        return pltpu.make_async_remote_copy(
            src_ref=src, dst_ref=dst, send_sem=send, recv_sem=recv,
            device_id=target, device_id_type=MESH,
        )

    quarters = [pl.ds(256 * i, 256) for i in range(4)]
    pairs = [(tok_hbm.at[:, at], tok_v.at[:, at]) for at in quarters]
    pairs += [(cot_hbm.at[:, at], cot_v.at[:, at]) for at in quarters]
    pairs += [(m_hbm, own_mv.at[0]), (v_hbm, own_mv.at[1]), (w_hbm, w_v)]
    loads = [pltpu.make_async_copy(src, dst, in_sem.at[i]) for i, (src, dst) in enumerate(pairs)]
    for load in loads[:10]:
        load.start()

    barrier = pltpu.get_barrier_semaphore()
    partners = (
        [at_y(d) for d in range(1, NY)]
        + [at_z(d) for d in range(1, NZ)]
        + [at_x(d) for d in range(1, NX)]
        + [far(ex) for ex in FAR]
        + [sibling]
    )
    for partner in partners:
        pl.semaphore_signal(barrier, inc=1, device_id=partner, device_id_type=MESH)

    for j in range(D // 128):
        lanes = slice(128 * j, 128 * j + 128)
        if j % 2 == 0:
            loads[j // 2].wait()
        tth[lanes, :], ttl[lanes, :] = split(tok_v[:, lanes].T * (1.0 / T))
    for j in range(D // 256):
        lanes = slice(256 * j, 256 * j + 256)
        loads[4 + j].wait()
        ch[:, lanes], cl[:, lanes] = split(cot_v[:, lanes])
    loads[8].wait()
    loads[9].wait()
    loads[10].start()
    pl.semaphore_wait(barrier, len(partners))

    mv_copy = remote(own_mv, sib_mv, cs_sem.at[1], cr_sem.at[1], sibling)
    mv_copy.start()

    def y_copy(b, s, d):
        rows = pl.ds(2 * b, 2)
        return remote(
            g.at[s, d, rows], yr.at[d - 1, s, rows],
            ys_sem.at[b, d - 1, s], yr_sem.at[b, d - 1, s], at_y(d),
        )

    def y_half(i, d):
        rows = pl.ds(2 + i, 1)
        return remote(
            g.at[NZ - 2, d, rows], yr.at[d - 1, NZ - 2, rows],
            yhs_sem.at[i, d - 1], yhr_sem.at[i, d - 1], at_y(d),
        )

    def z_half(i):
        rows = pl.ds(2 + i, 1)
        return remote(
            zs.at[NZ - 2, rows], zr.at[NZ - 2, rows], zhs_sem.at[i], zhr_sem.at[i], at_z(NZ - 1)
        )

    def z_copy(b, s, d):
        rows = pl.ds(2 * b, 2)
        return remote(
            zs.at[s, rows], zr.at[d - 1, rows], zs_sem.at[b, d - 1], zr_sem.at[b, d - 1], at_z(d)
        )

    def gradient_step(s, carry):
        owner = (z + offset_of(s)) % NZ
        starts = [
            pl.multiple_of((y + d) % NY * (D // NY) + owner * CH, CH) for d in range(NY)
        ]
        high = [tth[pl.ds(start, CH), :] for start in starts]
        low = [ttl[pl.ds(start, CH), :] for start in starts]
        count = NY * CH
        both = dot(jnp.concatenate(high + low, axis=0), ch[...], ((1,), (0,)))
        rest = dot(jnp.concatenate(high, axis=0), cl[...], ((1,), (0,)))
        value = both[:count] + both[count:] + rest
        for d in range(NY):
            for i in range(NX):
                at = d * CH + 8 * i
                g[s, d, 2 * (i % 2) + i // 2] = value[at : at + 8]
        for d in (2, 1, 3):
            y_copy(0, s, d).start()
        return carry

    lax.fori_loop(0, NZ, gradient_step, 0)

    def second_sends(s, carry):
        for d in (2, 1, 3):
            y_copy(1, s, d).start()
        return carry

    lax.fori_loop(0, NZ - 2, second_sends, 0)
    for i in range(2):
        for d in (2, 1, 3):
            y_half(i, d).start()
    second_sends(NZ - 1, 0)

    for j in range(D // 128):
        lanes = slice(128 * j, 128 * j + 128)
        piece = tok_v[:, lanes]
        th[:, lanes], tl[:, lanes] = split(piece)
        turned = piece.T.reshape(4, NX, 8, T)
        plane, quarter = j // 2, j % 2
        for b in range(2):
            at = (2 * b + plane % 2) * 256 + plane // 2 * 128 + quarter * 64
            ttp[at : at + 64] = jnp.stack([turned[:, b], turned[:, b + 2]], axis=1).reshape(64, T)
    loads[10].wait()

    def y_step(b, s):
        for d in range(1, NY):
            y_copy(b, s, d).wait_recv()
        rows = pl.ds(2 * b, 2)
        across = combine(g[s, 0, rows], yr[1, s, rows])
        zs[s, rows] = combine(across, combine(yr[0, s, rows], yr[2, s, rows]))
        z_copy(b, s, offset_of(s)).start()

    def y_step_halves():
        s = NZ - 2
        for i in range(2):
            for d in range(1, NY):
                y_half(i, d).wait_recv()
            q = 2 + i
            across = combine(g[s, 0, q], yr[1, s, q])
            zs[s, q] = combine(across, combine(yr[0, s, q], yr[2, s, q]))
            z_half(i).start()

    def filler(s):
        @pl.when(s < 4)
        def _():
            lanes = pl.ds(pl.multiple_of(s * 256, 256), 256)
            wh, wl = split(w_v[:, lanes])
            proj_v[:, lanes] = dot3(th[...], tl[...], wh, wl, ((1,), (0,)))

        @pl.when(s >= 4)
        def _():
            lanes = pl.ds(pl.multiple_of((s - 4) * 256, 256), 256)
            wh, wl = split(w_v[lanes, :])
            igrad_v[:, lanes] = dot3(ch[...], cl[...], wh, wl, ((1,), (1,)))

    def first_step(s, carry):
        y_step(0, s)
        filler(s)
        return carry

    lax.fori_loop(0, NZ - 1, first_step, 0)

    def z_pair(b, d):
        for at in (d, d + 4):
            z_copy(b, 0, at).wait_recv()
        rows = pl.ds(2 * b, 2)
        return combine(zr[d - 1, rows], zr[d + 3, rows])

    def x_copy(b, d):
        return remote(
            xs.at[b, d], xr.at[b, d - 1], xs_sem.at[b, d - 1], xr_sem.at[b, d - 1], at_x(d)
        )

    def reduce_sends(b):
        zz[b, 0] = z_pair(b, 2)
        zz[b, 1] = z_pair(b, 1)
        for d in (3, 4):
            z_copy(b, 0, d).wait_recv()
        if b == 0:
            z_copy(b, 0, 7).wait_recv()
        last = NZ - 1
        for d in range(1, NY):
            y_copy(b, last, d).wait_recv()

        def early(d):
            h = (x + d) % NX // 2
            q = 2 * b + h
            across = combine(g[last, 0, q], yr[1, last, q])
            across = combine(across, combine(yr[0, last, q], yr[2, last, q]))
            xs[b, d] = combine(combine(across, zr[3, q]), zz[b, 0, h])

        def late(d):
            h = (x + d) % NX // 2
            q = 2 * b + h
            if b == 1:
                z_half(h).wait_recv()
            rest = combine(zz[b, 1, h], combine(zr[2, q], zr[6, q]))
            xs[b, d] = combine(xs[b, d], rest)

        @pl.when(owns[b])
        def _():
            early(2)
            early(0)
            late(2)
            x_copy(b, 2).start()
            late(0)

        @pl.when(others[b])
        def _():
            early(1)
            early(3)
            for d in (1, 3):
                late(d)
                x_copy(b, d).start()

    c_copy = remote(cs, cr, cs_sem.at[0], cr_sem.at[0], sibling)

    def gather_rows(b):
        for d in range(1, NX):
            x_copy(b, d).wait_recv()
        cs[...] = combine(combine(xs[b, 0], xr[b, 1]), combine(xr[b, 0], xr[b, 2]))
        c_copy.start()

    half = D // 2
    mine_at = pl.multiple_of(c * half, half)
    mine_cols = pl.ds(mine_at, half)
    a_cols = pl.ds(mine_at, half // 2)
    b_cols = pl.ds(pl.multiple_of(mine_at + half // 2, half // 2), half // 2)
    a0_cols = pl.ds(mine_at, half - SIDE)
    b0_cols = pl.ds(pl.multiple_of(mine_at + half - SIDE, 128), SIDE)
    far_order = (4, 3, 5, 2, 6, 1, 7)
    order = [3, 1, 2]
    neighbours = [at_x(1), at_x(3), at_y(1), at_y(3)]

    def same(view, send, recv, target):
        return remote(view, view, send, recv, target)

    def z_block(d, target):
        view = wbuf.at[y, (z + d) % NZ, x, :, mine_cols]
        return same(view, gzs_sem.at[target - 1], gzr_sem.at[target - 1], at_z(target))

    def block(ey, ex, cols):
        return wbuf.at[(y + ey) % NY, :, (x + ex) % NX, :, cols]

    def sib_copy(ey, ex, column_start):
        cols = pl.ds(pl.multiple_of(column_start, half), half)
        return same(block(ey, ex, cols), gss_sem.at[ey, ex], gsr_sem.at[ey, ex], sibling)

    def to_sibling(ey, ex):
        sib_copy(ey, ex, mine_at).start()

    def update_rows():
        mv_copy.wait()
        mine, other = own_mv[...], sib_mv[...]
        first = c == 0
        lower, upper = jnp.where(first, mine, other), jnp.where(first, other, mine)
        moments = [jnp.concatenate([lower[i], upper[i]], axis=0) for i in range(2)]
        old_rows = w_v[pl.ds(pl.multiple_of(me // 2 * 8, 8), 8), :]
        c_copy.wait()
        summed = combine(cs[...], cr[...])
        new_rows, new_first, new_second = adam_update(summed, old_rows, moments[0], moments[1])
        wbuf[y, z, x, :, mine_cols] = jnp.where(first, new_rows[:, :half], new_rows[:, half:])
        for d in far_order:
            z_block(0, d).start()
        return first, new_first, new_second

    def keep_moments(first, new_first, new_second):
        m_v[...] = jnp.where(first, new_first[:4], new_first[4:])
        v_v[...] = jnp.where(first, new_second[:4], new_second[4:])

    def x_column(d, ex):
        return same(block(0, ex, mine_cols), gxs_sem.at[d - 1], gxr_sem.at[d - 1], at_x(d))

    def y_column(k, e, ey, ex):
        i = 3 * k + e - 1
        cols = mine_cols if ex % 2 == 0 else a0_cols
        return same(block(ey, ex, cols), gys_sem.at[i], gyr_sem.at[i], at_y(e))

    def y_side(e, d, ex):
        i = 3 * (e - 1) + d - 1
        return same(block(NY - e, ex, b0_cols), y0s_sem.at[i], y0r_sem.at[i], at_x(d))

    def turn(i):
        at = slice(256 * i, 256 * i + 256)
        thp[:, at], tlp[:, at] = split(ttp[at, :].T)

    def following(b, pair, columns):
        for ey in (pair, pair + 2):
            for ex in columns:
                sib_copy(ey, ex, (1 - c) * half).wait_recv()
        p = (y + pair) % 2
        parts = [
            jnp.stack([wbuf[p + 2 * i, :, b], wbuf[p + 2 * i, :, b + 2]], axis=1).reshape(128, D)
            for i in range(2)
        ]
        lanes = pl.ds(pl.multiple_of((2 * b + p) * 256, 256), 256)
        wh, wl = split(jnp.concatenate(parts, axis=0))
        return dot3(thp[:, lanes], tlp[:, lanes], wh, wl, ((1,), (0,)))

    filler(NZ - 1)
    reduce_sends(0)
    for s in range(NZ - 1):
        if s < NZ - 2:
            y_step(1, s)
        else:
            y_step_halves()
        if s in (1, 3, 5, 6):
            turn((1, 3, 5, 6).index(s))
        if s == 1:

            @pl.when(even)
            def _():
                gather_rows(0)

        if s == 2:

            @pl.when(even)
            def _():
                keep_moments(*update_rows())

        if s == 4:

            @pl.when(even)
            def _():
                for d in far_order:
                    z_block(NZ - d, d).wait_recv()
                for d in (2, 1, 3):
                    x_column(d, 0).start()
                to_sibling(0, 0)

    reduce_sends(1)

    def far_block(j, d):
        return wbuf.at[(y + 2) % NY, (z + d) % NZ, (x + NX - FAR[j]) % NX, :, mine_cols]

    def far_first(j):
        return same(far_block(j, 0), fis_sem.at[j], fir_sem.at[j], far(FAR[j]))

    def far_copy(j, at, d):
        i = j * (NZ - 1) + d - 1
        return same(far_block(j, at), fzs_sem.at[i], fzr_sem.at[i], at_z(d))

    def two_away(i, ey, ex):
        target = at_x(2) if i == 0 else at_y(2)
        return same(block(ey, ex, mine_cols), g2s_sem.at[i], g2r_sem.at[i], target)

    def from_neighbour(i):
        ey, ex = [(0, 3), (0, 1), (3, 0), (1, 0)][i]
        return same(block(ey, ex, mine_cols), gns_sem.at[i], gnr_sem.at[i], neighbours[i])

    def a_flow(k, direction, ey):
        i = 2 * k + direction
        return same(block(ey, order[k], a_cols), gas_sem.at[i], gar_sem.at[i], neighbours[2 + direction])

    def b_flow(k, target, ex):
        i = 3 * k + target
        return same(
            block(order[k], ex, b_cols), gbs_sem.at[i], gbr_sem.at[i], at_x((1, 3, 2)[target])
        )

    def y_column_out(k, ex):
        for e in (2, 1, 3):
            y_column(k, e, 0, ex).start()

    def y_column_in(k, ex, d):
        for e in (1, 3, 2):
            y_column(k, e, NY - e, ex).wait_recv()
            if d != 2:
                y_side(e, d, ex).wait_recv()
            to_sibling(NY - e, ex)

    def far_in(js):
        for j in js:
            far_first(j).wait_recv()
            for d in far_order:
                far_copy(j, 0, d).start()

    def far_columns_in(js):
        for j in js:
            for d in far_order:
                far_copy(j, NZ - d, d).wait_recv()
            to_sibling(2, NX - FAR[j])

    def drain(columns, own, js, as_, bs):
        for k, ex in enumerate(columns):
            for e in range(1, NY):
                y_column(k, e, 0, ex).wait_send()
        for d in range(1, NZ):
            z_block(0, d).wait_send()
            for j in js:
                far_copy(j, 0, d).wait_send()
        for k, direction in as_:
            a_flow(k, direction, 0).wait_send()
        for k, target in bs:
            b_flow(k, target, 0).wait_send()

    @pl.when(odd)
    def _():
        def to_neighbours(d):
            view = wbuf.at[y, (z + d) % NZ, x, :, mine_cols]
            for i, target in enumerate(neighbours):
                same(view, gns_sem.at[i], gnr_sem.at[i], target).start()
            same(view, g2s_sem.at[0], g2r_sem.at[0], at_x(2)).start()

        x_column(1, 3).wait_recv()
        x_column(3, 1).wait_recv()
        y_column_out(0, 3)
        y_column_out(1, 1)
        to_sibling(0, 3)
        to_sibling(0, 1)
        gather_rows(1)
        updated = update_rows()
        for i in range(3):
            same(wbuf.at[y, z, x, :, mine_cols], fis_sem.at[i], fir_sem.at[i], far(FAR[i])).start()
        to_neighbours(0)
        keep_moments(*updated)
        for d in (1, 7, 2, 6, 3, 5, 4):
            z_block(NZ - d, d).wait_recv()
            to_neighbours(NZ - d)
        two_away(1, 0, 0).start()
        far_in((0,))
        to_sibling(0, 0)
        for k in range(2):
            from_neighbour(2 + k).wait_recv()
            for target in (0, 1, 2):
                b_flow(k, target, 0).start()
            to_sibling(order[k], 0)
        two_away(0, 0, 2).wait_recv()
        for direction in range(2):
            a_flow(2, direction, 0).start()
        to_sibling(0, 2)
        y_column_in(0, 3, 1)
        y_column_in(1, 1, 3)
        two_away(1, 2, 0).wait_recv()
        to_sibling(2, 0)
        far_columns_in((0,))
        next_v[...] = following(0, 0, (3, 1))
        next_v[...] += following(0, 1, (3, 1))
        next_v[...] += following(1, 0, (0, 2))
        for direction in range(2):
            a_flow(2, direction, order[direction]).wait_recv()
            b_flow(direction, 2, 2).wait_recv()
            to_sibling(order[direction], 2)
        next_v[...] += following(1, 1, (0, 2))
        for i in range(3):
            same(wbuf.at[y, z, x, :, mine_cols], fis_sem.at[i], fir_sem.at[i], far(FAR[i])).wait_send()
        for i in range(4):
            from_neighbour(i).wait_send()
        for i in range(2):
            two_away(i, 0, 0).wait_send()
        for d in (1, 3):
            x_copy(0, d).wait_send()
        x_copy(1, 2).wait_send()
        drain(
            (3, 1), True, (0,), [(2, 0), (2, 1)], [(k, t) for k in range(2) for t in range(3)]
        )

    @pl.when(even)
    def _():
        x_column(2, 2).wait_recv()
        y_column_out(0, 0)
        y_column_out(1, 2)
        to_sibling(0, 2)
        for e in (1, 3, 2):
            y_column(0, e, NY - e, 0).wait_recv()
            for d in (1, 3):
                y_side(e, d, 0).start()
            to_sibling(NY - e, 0)
        far_in((1, 2))
        for k in range(2):
            from_neighbour(k).wait_recv()
            for direction in range(2):
                a_flow(k, direction, 0).start()
            to_sibling(0, order[k])
        y_column_in(1, 2, 2)
        far_columns_in((1, 2))
        next_v[...] = following(0, 0, (0, 2))
        next_v[...] += following(0, 1, (0, 2))
        next_v[...] += following(1, 0, (3, 1))
        for k in range(2):
            for direction in range(2):
                a_flow(k, direction, order[direction]).wait_recv()
                b_flow(direction, k, order[k]).wait_recv()
                to_sibling(order[direction], order[k])
        next_v[...] += following(1, 1, (3, 1))
        for d in range(1, NX):
            x_column(d, 0).wait_send()
            if d != 2:
                for e in range(1, NY):
                    y_side(e, d, 0).wait_send()
        for d in (1, 3):
            x_copy(1, d).wait_send()
        x_copy(0, 2).wait_send()
        drain((0, 2), False, (1, 2), [(k, i) for k in range(2) for i in range(2)], [])

    def y_drain(s, carry):
        for d in range(1, NY):
            y_copy(0, s, d).wait_send()

        @pl.when(s != NZ - 2)
        def _():
            for d in range(1, NY):
                y_copy(1, s, d).wait_send()

        return carry

    lax.fori_loop(0, NZ, y_drain, 0)
    for i in range(2):
        for d in range(1, NY):
            y_half(i, d).wait_send()
        z_half(i).wait_send()
    for d in range(1, NZ):
        z_copy(0, 0, d).wait_send()
    for d in range(1, NZ - 1):
        z_copy(1, 0, d).wait_send()
    for ey in range(NY):
        for ex in range(NX):
            sib_copy(ey, ex, mine_at).wait_send()


PIECES = (2, 2, 2, 4, 1, 1)


def store_kernel(*refs):
    sources, targets, sem = refs[:6], refs[6:12], refs[12]
    copies = []
    for i, (source, target) in enumerate(zip(sources, targets)):
        count = PIECES[i]
        size = source.shape[0] // count
        for j in range(count):
            rows = pl.ds(j * size, size)
            copies.append(pltpu.make_async_copy(source.at[rows], target.at[rows], sem.at[len(copies)]))
    for copy in copies:
        copy.start()
    for copy in copies:
        copy.wait()


def on_device(tokens, cotangent, weight, first_moment, second_moment):
    dma = pltpu.SemaphoreType.DMA
    any_space = pl.BlockSpec(memory_space=pl.ANY)
    rows = lambda *shape: pltpu.VMEM(shape + (D,), F32)
    shapes = [(T, D), (T, D), (T, D), (NY, NZ, NX, 8, D), (4, D), (4, D)]
    held = pl.pallas_call(
        exchange_kernel,
        out_shape=[pltpu.VMEM(shape, F32) for shape in shapes],
        in_specs=[any_space] * 5,
        out_specs=[pl.BlockSpec(memory_space=pltpu.VMEM)] * 6,
        scratch_shapes=[
            rows(T), rows(T), rows(D),
            pltpu.VMEM((D, T), BF16), pltpu.VMEM((D, T), BF16), pltpu.VMEM((D, T), F32),
            pltpu.VMEM((T, D), BF16), pltpu.VMEM((T, D), BF16),
            pltpu.VMEM((T, D), BF16), pltpu.VMEM((T, D), BF16),
            pltpu.VMEM((T, D), BF16), pltpu.VMEM((T, D), BF16),
            rows(NZ, NY, NX, 8), rows(NY - 1, NZ, NX, 8),
            rows(NZ, NX, 8), rows(NZ - 1, NX, 8), rows(2, 2, 2, 8),
            rows(2, NX, 8), rows(2, NX - 1, 8), rows(8), rows(8),
            rows(2, 4), rows(2, 4),
            dma((11,)), dma((2, NY - 1)), dma((2, NY - 1)), dma((2,)), dma((2,)),
            dma((2, NY - 1, NZ)), dma((2, NY - 1, NZ)), dma((2, NZ - 1)), dma((2, NZ - 1)),
            dma((2, NX - 1)), dma((2, NX - 1)), dma((2,)), dma((2,)),
            dma((NZ - 1,)), dma((NZ - 1,)), dma((NX - 1,)), dma((NX - 1,)),
            dma((6,)), dma((6,)), dma((4,)), dma((4,)), dma((2,)), dma((2,)),
            dma((9,)), dma((9,)), dma((3,)), dma((3,)), dma((3 * (NZ - 1),)), dma((3 * (NZ - 1),)),
            dma((6,)), dma((6,)), dma((6,)), dma((6,)),
            dma((NY, NX)), dma((NY, NX)),
        ],
        compiler_params=pltpu.CompilerParams(
            collective_id=0, has_side_effects=True, vmem_limit_bytes=52 * 2**20
        ),
        name="exchange",
    )(tokens, cotangent, weight, first_moment, second_moment)
    projected, input_grad, next_projected, new_weight, new_first, new_second = pl.pallas_call(
        store_kernel,
        out_shape=[jax.ShapeDtypeStruct(shape, F32) for shape in shapes],
        in_specs=[any_space] * 6,
        out_specs=[pl.BlockSpec(memory_space=pltpu.HBM)] * 6,
        scratch_shapes=[dma((sum(PIECES),))],
        compiler_params=pltpu.CompilerParams(vmem_limit_bytes=2**20),
        name="store",
    )(*held)
    new_weight = new_weight.reshape(D, D)
    return (projected, input_grad, new_weight, new_first, new_second, next_projected)


def solution(mesh):
    placed = (P("dp", None), P("dp", None), P(), P("dp", None), P("dp", None))
    return jax.shard_map(
        on_device,
        mesh=mesh,
        in_specs=placed,
        out_specs=(P("dp", None), P("dp", None), P(), P("dp", None), P("dp", None), P("dp", None)),
        check_vma=False,
    )
```

```python
import jax
import jax.numpy as jnp
from jax import lax
from jax.experimental import pallas as pl
from jax.experimental.pallas import tpu as pltpu
from jax.sharding import PartitionSpec as P

beta_one = 0.9
beta_two = 0.999
rate_value = 0.01
step_count = 10
adam_epsilon = 1e-08
norm_epsilon = 1e-06

MESH = pl.DeviceIdType.MESH
NY, NZ, NX = 4, 8, 4
D = 1024
T = 256
CH = D // (NY * NZ)
FAR = (2, 1, 3)
SIDE = 256
F32, BF16 = jnp.float32, jnp.bfloat16


def combine(left_rows, right_rows):
    cross_term = jnp.sum(left_rows * right_rows, axis=-1, keepdims=True)
    left_norm = jnp.sum(left_rows * left_rows, axis=-1, keepdims=True)
    right_norm = jnp.sum(right_rows * right_rows, axis=-1, keepdims=True)
    left_coef = 1.0 - cross_term / (2.0 * (left_norm + norm_epsilon))
    right_coef = 1.0 - cross_term / (2.0 * (right_norm + norm_epsilon))
    return left_coef * left_rows + right_coef * right_rows


def adam_update(gradient, weight_rows, first_rows, second_rows):
    first_new = beta_one * first_rows + (1.0 - beta_one) * gradient
    second_new = beta_two * second_rows + (1.0 - beta_two) * gradient * gradient
    first_hat = first_new / (1.0 - beta_one**step_count)
    second_hat = second_new / (1.0 - beta_two**step_count)
    weight_new = weight_rows - rate_value * first_hat / (jnp.sqrt(second_hat) + adam_epsilon)
    return (weight_new, first_new, second_new)


def split(value):
    high = value.astype(BF16)
    return high, (value - high.astype(F32)).astype(BF16)


def dot(a, b, contract):
    return lax.dot_general(a, b, (contract, ((), ())), preferred_element_type=F32)


def dot3(a_high, a_low, b_high, b_low, contract):
    return (
        dot(a_high, b_high, contract)
        + dot(a_high, b_low, contract)
        + dot(a_low, b_high, contract)
    )


def offset_of(s):
    return 4 + (s + 1) // 2 * (1 - 2 * (s % 2))


def exchange_kernel(
    tok_hbm, cot_hbm, w_hbm, m_hbm, v_hbm,
    proj_v, igrad_v, next_v, wbuf, m_v, v_v,
    tok_v, cot_v, w_v, tth, ttl, ttp, th, tl, thp, tlp, ch, cl,
    g, yr, zs, zr, zz, xs, xr, cs, cr, own_mv, sib_mv,
    in_sem, yhs_sem, yhr_sem, zhs_sem, zhr_sem, ys_sem, yr_sem, zs_sem, zr_sem, xs_sem, xr_sem, cs_sem, cr_sem,
    gzs_sem, gzr_sem, gxs_sem, gxr_sem, gys_sem, gyr_sem, gns_sem, gnr_sem, g2s_sem, g2r_sem,
    y0s_sem, y0r_sem, fis_sem, fir_sem, fzs_sem, fzr_sem, gas_sem, gar_sem, gbs_sem, gbr_sem, gss_sem, gsr_sem,
):
    me = lax.axis_index("dp")
    c = me % 2
    x = me // 2 % NX
    z = me // (2 * NX) % NZ
    y = me // (2 * NX * NZ)
    odd = x % 2 == 1
    even = x % 2 == 0
    owns = [even, odd]
    others = [odd, even]

    def device(yy, zz, xx, cc):
        return (((yy * NZ + zz) * NX + xx) * 2 + cc,)

    def at_y(d):
        return device((y + d) % NY, z, x, c)

    def at_z(d):
        return device(y, (z + d) % NZ, x, c)

    def at_x(d):
        return device(y, z, (x + d) % NX, c)

    sibling = device(y, z, x, 1 - c)

    def far(ex):
        return device((y + 2) % NY, z, (x + ex) % NX, c)

    def remote(src, dst, send, recv, target):
        return pltpu.make_async_remote_copy(
            src_ref=src, dst_ref=dst, send_sem=send, recv_sem=recv,
            device_id=target, device_id_type=MESH,
        )

    quarters = [pl.ds(256 * i, 256) for i in range(4)]
    pairs = [(tok_hbm.at[:, at], tok_v.at[:, at]) for at in quarters]
    pairs += [(cot_hbm.at[:, at], cot_v.at[:, at]) for at in quarters]
    pairs += [(m_hbm, own_mv.at[0]), (v_hbm, own_mv.at[1]), (w_hbm, w_v)]
    loads = [pltpu.make_async_copy(src, dst, in_sem.at[i]) for i, (src, dst) in enumerate(pairs)]
    for load in loads[:10]:
        load.start()

    barrier = pltpu.get_barrier_semaphore()
    partners = (
        [at_y(d) for d in range(1, NY)]
        + [at_z(d) for d in range(1, NZ)]
        + [at_x(d) for d in range(1, NX)]
        + [far(ex) for ex in FAR]
        + [sibling]
    )
    for partner in partners:
        pl.semaphore_signal(barrier, inc=1, device_id=partner, device_id_type=MESH)

    for j in range(D // 128):
        lanes = slice(128 * j, 128 * j + 128)
        if j % 2 == 0:
            loads[j // 2].wait()
        tth[lanes, :], ttl[lanes, :] = split(tok_v[:, lanes].T * (1.0 / T))
    for j in range(D // 256):
        lanes = slice(256 * j, 256 * j + 256)
        loads[4 + j].wait()
        ch[:, lanes], cl[:, lanes] = split(cot_v[:, lanes])
    loads[10].start()
    pl.semaphore_wait(barrier, len(partners))

    def y_copy(b, s, d):
        rows = pl.ds(2 * b, 2)
        return remote(
            g.at[s, d, rows], yr.at[d - 1, s, rows],
            ys_sem.at[b, d - 1, s], yr_sem.at[b, d - 1, s], at_y(d),
        )

    def y_half(i, d):
        rows = pl.ds(2 + i, 1)
        return remote(
            g.at[NZ - 2, d, rows], yr.at[d - 1, NZ - 2, rows],
            yhs_sem.at[i, d - 1], yhr_sem.at[i, d - 1], at_y(d),
        )

    def z_half(i):
        rows = pl.ds(2 + i, 1)
        return remote(
            zs.at[NZ - 2, rows], zr.at[NZ - 2, rows], zhs_sem.at[i], zhr_sem.at[i], at_z(NZ - 1)
        )

    def z_copy(b, s, d):
        rows = pl.ds(2 * b, 2)
        return remote(
            zs.at[s, rows], zr.at[d - 1, rows], zs_sem.at[b, d - 1], zr_sem.at[b, d - 1], at_z(d)
        )

    def gradient_step(s, carry):
        owner = (z + offset_of(s)) % NZ
        starts = [
            pl.multiple_of((y + d) % NY * (D // NY) + owner * CH, CH) for d in range(NY)
        ]
        high = [tth[pl.ds(start, CH), :] for start in starts]
        low = [ttl[pl.ds(start, CH), :] for start in starts]
        count = NY * CH
        both = dot(jnp.concatenate(high + low, axis=0), ch[...], ((1,), (0,)))
        rest = dot(jnp.concatenate(high, axis=0), cl[...], ((1,), (0,)))
        value = both[:count] + both[count:] + rest
        for d in range(NY):
            for i in range(NX):
                at = d * CH + 8 * i
                g[s, d, 2 * (i % 2) + i // 2] = value[at : at + 8]
        for d in (2, 1, 3):
            y_copy(0, s, d).start()
        return carry

    lax.fori_loop(0, NZ, gradient_step, 0)

    def second_sends(s, carry):
        for d in (2, 1, 3):
            y_copy(1, s, d).start()
        return carry

    lax.fori_loop(0, NZ - 2, second_sends, 0)
    for i in range(2):
        for d in (2, 1, 3):
            y_half(i, d).start()
    second_sends(NZ - 1, 0)

    loads[8].wait()
    loads[9].wait()
    mv_copy = remote(own_mv, sib_mv, cs_sem.at[1], cr_sem.at[1], sibling)
    mv_copy.start()

    for j in range(D // 128):
        lanes = slice(128 * j, 128 * j + 128)
        piece = tok_v[:, lanes]
        th[:, lanes], tl[:, lanes] = split(piece)
        turned = piece.T.reshape(4, NX, 8, T)
        plane, quarter = j // 2, j % 2
        for b in range(2):
            at = (2 * b + plane % 2) * 256 + plane // 2 * 128 + quarter * 64
            ttp[at : at + 64] = jnp.stack([turned[:, b], turned[:, b + 2]], axis=1).reshape(64, T)
    loads[10].wait()

    def y_step(b, s):
        for d in range(1, NY):
            y_copy(b, s, d).wait_recv()
        rows = pl.ds(2 * b, 2)
        across = combine(g[s, 0, rows], yr[1, s, rows])
        zs[s, rows] = combine(across, combine(yr[0, s, rows], yr[2, s, rows]))
        z_copy(b, s, offset_of(s)).start()

    def y_step_halves():
        s = NZ - 2
        for i in range(2):
            for d in range(1, NY):
                y_half(i, d).wait_recv()
            q = 2 + i
            across = combine(g[s, 0, q], yr[1, s, q])
            zs[s, q] = combine(across, combine(yr[0, s, q], yr[2, s, q]))
            z_half(i).start()

    def filler(s):
        @pl.when(s < 4)
        def _():
            lanes = pl.ds(pl.multiple_of(s * 256, 256), 256)
            wh, wl = split(w_v[:, lanes])
            proj_v[:, lanes] = dot3(th[...], tl[...], wh, wl, ((1,), (0,)))

        @pl.when(s >= 4)
        def _():
            lanes = pl.ds(pl.multiple_of((s - 4) * 256, 256), 256)
            wh, wl = split(w_v[lanes, :])
            igrad_v[:, lanes] = dot3(ch[...], cl[...], wh, wl, ((1,), (1,)))

    def first_step(s, carry):
        y_step(0, s)
        filler(s)
        return carry

    lax.fori_loop(0, NZ - 1, first_step, 0)

    def z_pair(b, d):
        for at in (d, d + 4):
            z_copy(b, 0, at).wait_recv()
        rows = pl.ds(2 * b, 2)
        return combine(zr[d - 1, rows], zr[d + 3, rows])

    def x_copy(b, d):
        return remote(
            xs.at[b, d], xr.at[b, d - 1], xs_sem.at[b, d - 1], xr_sem.at[b, d - 1], at_x(d)
        )

    def reduce_sends(b):
        zz[b, 0] = z_pair(b, 2)
        zz[b, 1] = z_pair(b, 1)
        for d in (3, 4):
            z_copy(b, 0, d).wait_recv()
        if b == 0:
            z_copy(b, 0, 7).wait_recv()
        last = NZ - 1
        for d in range(1, NY):
            y_copy(b, last, d).wait_recv()

        def early(d):
            h = (x + d) % NX // 2
            q = 2 * b + h
            across = combine(g[last, 0, q], yr[1, last, q])
            across = combine(across, combine(yr[0, last, q], yr[2, last, q]))
            xs[b, d] = combine(combine(across, zr[3, q]), zz[b, 0, h])

        def late(d):
            h = (x + d) % NX // 2
            q = 2 * b + h
            if b == 1:
                z_half(h).wait_recv()
            rest = combine(zz[b, 1, h], combine(zr[2, q], zr[6, q]))
            xs[b, d] = combine(xs[b, d], rest)

        @pl.when(owns[b])
        def _():
            early(2)
            early(0)
            late(2)
            x_copy(b, 2).start()
            late(0)

        @pl.when(others[b])
        def _():
            early(1)
            early(3)
            for d in (1, 3):
                late(d)
                x_copy(b, d).start()

    c_copy = remote(cs, cr, cs_sem.at[0], cr_sem.at[0], sibling)

    def gather_rows(b):
        for d in range(1, NX):
            x_copy(b, d).wait_recv()
        cs[...] = combine(combine(xs[b, 0], xr[b, 1]), combine(xr[b, 0], xr[b, 2]))
        c_copy.start()

    half = D // 2
    mine_at = pl.multiple_of(c * half, half)
    mine_cols = pl.ds(mine_at, half)
    a_cols = pl.ds(mine_at, half // 2)
    b_cols = pl.ds(pl.multiple_of(mine_at + half // 2, half // 2), half // 2)
    a0_cols = pl.ds(mine_at, half - SIDE)
    b0_cols = pl.ds(pl.multiple_of(mine_at + half - SIDE, 128), SIDE)
    far_order = (4, 3, 5, 2, 6, 1, 7)
    order = [3, 1, 2]
    neighbours = [at_x(1), at_x(3), at_y(1), at_y(3)]

    def same(view, send, recv, target):
        return remote(view, view, send, recv, target)

    def z_block(d, target):
        view = wbuf.at[y, (z + d) % NZ, x, :, mine_cols]
        return same(view, gzs_sem.at[target - 1], gzr_sem.at[target - 1], at_z(target))

    def block(ey, ex, cols):
        return wbuf.at[(y + ey) % NY, :, (x + ex) % NX, :, cols]

    def sib_copy(ey, ex, column_start):
        cols = pl.ds(pl.multiple_of(column_start, half), half)
        return same(block(ey, ex, cols), gss_sem.at[ey, ex], gsr_sem.at[ey, ex], sibling)

    def to_sibling(ey, ex):
        sib_copy(ey, ex, mine_at).start()

    def update_rows():
        mv_copy.wait()
        mine, other = own_mv[...], sib_mv[...]
        first = c == 0
        lower, upper = jnp.where(first, mine, other), jnp.where(first, other, mine)
        moments = [jnp.concatenate([lower[i], upper[i]], axis=0) for i in range(2)]
        old_rows = w_v[pl.ds(pl.multiple_of(me // 2 * 8, 8), 8), :]
        c_copy.wait()
        summed = combine(cs[...], cr[...])
        new_rows, new_first, new_second = adam_update(summed, old_rows, moments[0], moments[1])
        wbuf[y, z, x, :, mine_cols] = jnp.where(first, new_rows[:, :half], new_rows[:, half:])
        for d in far_order:
            z_block(0, d).start()
        return first, new_first, new_second

    def keep_moments(first, new_first, new_second):
        m_v[...] = jnp.where(first, new_first[:4], new_first[4:])
        v_v[...] = jnp.where(first, new_second[:4], new_second[4:])

    def x_column(d, ex):
        return same(block(0, ex, mine_cols), gxs_sem.at[d - 1], gxr_sem.at[d - 1], at_x(d))

    def y_column(k, e, ey, ex):
        i = 3 * k + e - 1
        cols = mine_cols if ex % 2 == 0 else a0_cols
        return same(block(ey, ex, cols), gys_sem.at[i], gyr_sem.at[i], at_y(e))

    def y_side(e, d, ex):
        i = 3 * (e - 1) + d - 1
        return same(block(NY - e, ex, b0_cols), y0s_sem.at[i], y0r_sem.at[i], at_x(d))

    def turn(i):
        at = slice(256 * i, 256 * i + 256)
        thp[:, at], tlp[:, at] = split(ttp[at, :].T)

    def following(b, pair, columns):
        for ey in (pair, pair + 2):
            for ex in columns:
                sib_copy(ey, ex, (1 - c) * half).wait_recv()
        p = (y + pair) % 2
        parts = [
            jnp.stack([wbuf[p + 2 * i, :, b], wbuf[p + 2 * i, :, b + 2]], axis=1).reshape(128, D)
            for i in range(2)
        ]
        lanes = pl.ds(pl.multiple_of((2 * b + p) * 256, 256), 256)
        wh, wl = split(jnp.concatenate(parts, axis=0))
        return dot3(thp[:, lanes], tlp[:, lanes], wh, wl, ((1,), (0,)))

    filler(NZ - 1)
    reduce_sends(0)
    for s in range(NZ - 1):
        if s < NZ - 2:
            y_step(1, s)
        else:
            y_step_halves()
        if s in (1, 3, 5, 6):
            turn((1, 3, 5, 6).index(s))
        if s == 1:

            @pl.when(even)
            def _():
                gather_rows(0)

        if s == 2:

            @pl.when(even)
            def _():
                keep_moments(*update_rows())

        if s == 4:

            @pl.when(even)
            def _():
                for d in far_order:
                    z_block(NZ - d, d).wait_recv()
                for d in (2, 1, 3):
                    x_column(d, 0).start()
                to_sibling(0, 0)

    reduce_sends(1)

    def far_block(j, d):
        return wbuf.at[(y + 2) % NY, (z + d) % NZ, (x + NX - FAR[j]) % NX, :, mine_cols]

    def far_first(j):
        return same(far_block(j, 0), fis_sem.at[j], fir_sem.at[j], far(FAR[j]))

    def far_copy(j, at, d):
        i = j * (NZ - 1) + d - 1
        return same(far_block(j, at), fzs_sem.at[i], fzr_sem.at[i], at_z(d))

    def two_away(i, ey, ex):
        target = at_x(2) if i == 0 else at_y(2)
        return same(block(ey, ex, mine_cols), g2s_sem.at[i], g2r_sem.at[i], target)

    def from_neighbour(i):
        ey, ex = [(0, 3), (0, 1), (3, 0), (1, 0)][i]
        return same(block(ey, ex, mine_cols), gns_sem.at[i], gnr_sem.at[i], neighbours[i])

    def a_flow(k, direction, ey):
        i = 2 * k + direction
        return same(block(ey, order[k], a_cols), gas_sem.at[i], gar_sem.at[i], neighbours[2 + direction])

    def b_flow(k, target, ex):
        i = 3 * k + target
        return same(
            block(order[k], ex, b_cols), gbs_sem.at[i], gbr_sem.at[i], at_x((1, 3, 2)[target])
        )

    def y_column_out(k, ex):
        for e in (2, 1, 3):
            y_column(k, e, 0, ex).start()

    def y_column_in(k, ex, d):
        for e in (1, 3, 2):
            y_column(k, e, NY - e, ex).wait_recv()
            if d != 2:
                y_side(e, d, ex).wait_recv()
            to_sibling(NY - e, ex)

    def far_in(js):
        for j in js:
            far_first(j).wait_recv()
            for d in far_order:
                far_copy(j, 0, d).start()

    def far_columns_in(js):
        for j in js:
            for d in far_order:
                far_copy(j, NZ - d, d).wait_recv()
            to_sibling(2, NX - FAR[j])

    def drain(columns, own, js, as_, bs):
        for k, ex in enumerate(columns):
            for e in range(1, NY):
                y_column(k, e, 0, ex).wait_send()
        for d in range(1, NZ):
            z_block(0, d).wait_send()
            for j in js:
                far_copy(j, 0, d).wait_send()
        for k, direction in as_:
            a_flow(k, direction, 0).wait_send()
        for k, target in bs:
            b_flow(k, target, 0).wait_send()

    @pl.when(odd)
    def _():
        def to_neighbours(d):
            view = wbuf.at[y, (z + d) % NZ, x, :, mine_cols]
            for i, target in enumerate(neighbours):
                same(view, gns_sem.at[i], gnr_sem.at[i], target).start()

        x_column(1, 3).wait_recv()
        x_column(3, 1).wait_recv()
        y_column_out(0, 3)
        y_column_out(1, 1)
        to_sibling(0, 3)
        to_sibling(0, 1)
        gather_rows(1)
        updated = update_rows()
        for i in range(3):
            same(wbuf.at[y, z, x, :, mine_cols], fis_sem.at[i], fir_sem.at[i], far(FAR[i])).start()
        to_neighbours(0)
        keep_moments(*updated)
        for d in (1, 7, 2, 6, 3, 5, 4):
            z_block(NZ - d, d).wait_recv()
            to_neighbours(NZ - d)
        two_away(0, 0, 0).start()
        two_away(1, 0, 0).start()
        far_in((0,))
        to_sibling(0, 0)
        for k in range(2):
            from_neighbour(2 + k).wait_recv()
            for target in (0, 1, 2):
                b_flow(k, target, 0).start()
            to_sibling(order[k], 0)
        two_away(0, 0, 2).wait_recv()
        for direction in range(2):
            a_flow(2, direction, 0).start()
        to_sibling(0, 2)
        y_column_in(0, 3, 1)
        y_column_in(1, 1, 3)
        two_away(1, 2, 0).wait_recv()
        to_sibling(2, 0)
        far_columns_in((0,))
        next_v[...] = following(0, 0, (3, 1))
        next_v[...] += following(0, 1, (3, 1))
        next_v[...] += following(1, 0, (0, 2))
        for direction in range(2):
            a_flow(2, direction, order[direction]).wait_recv()
            b_flow(direction, 2, 2).wait_recv()
            to_sibling(order[direction], 2)
        next_v[...] += following(1, 1, (0, 2))
        for i in range(3):
            same(wbuf.at[y, z, x, :, mine_cols], fis_sem.at[i], fir_sem.at[i], far(FAR[i])).wait_send()
        for i in range(4):
            from_neighbour(i).wait_send()
        for i in range(2):
            two_away(i, 0, 0).wait_send()
        for d in (1, 3):
            x_copy(0, d).wait_send()
        x_copy(1, 2).wait_send()
        drain(
            (3, 1), True, (0,), [(2, 0), (2, 1)], [(k, t) for k in range(2) for t in range(3)]
        )

    @pl.when(even)
    def _():
        x_column(2, 2).wait_recv()
        y_column_out(0, 0)
        y_column_out(1, 2)
        to_sibling(0, 2)
        for e in (1, 3, 2):
            y_column(0, e, NY - e, 0).wait_recv()
            for d in (1, 3):
                y_side(e, d, 0).start()
            to_sibling(NY - e, 0)
        far_in((1, 2))
        for k in range(2):
            from_neighbour(k).wait_recv()
            for direction in range(2):
                a_flow(k, direction, 0).start()
            to_sibling(0, order[k])
        y_column_in(1, 2, 2)
        far_columns_in((1, 2))
        next_v[...] = following(0, 0, (0, 2))
        next_v[...] += following(0, 1, (0, 2))
        next_v[...] += following(1, 0, (3, 1))
        for k in range(2):
            for direction in range(2):
                a_flow(k, direction, order[direction]).wait_recv()
                b_flow(direction, k, order[k]).wait_recv()
                to_sibling(order[direction], order[k])
        next_v[...] += following(1, 1, (3, 1))
        for d in range(1, NX):
            x_column(d, 0).wait_send()
            if d != 2:
                for e in range(1, NY):
                    y_side(e, d, 0).wait_send()
        for d in (1, 3):
            x_copy(1, d).wait_send()
        x_copy(0, 2).wait_send()
        drain((0, 2), False, (1, 2), [(k, i) for k in range(2) for i in range(2)], [])

    def y_drain(s, carry):
        for d in range(1, NY):
            y_copy(0, s, d).wait_send()

        @pl.when(s != NZ - 2)
        def _():
            for d in range(1, NY):
                y_copy(1, s, d).wait_send()

        return carry

    lax.fori_loop(0, NZ, y_drain, 0)
    for i in range(2):
        for d in range(1, NY):
            y_half(i, d).wait_send()
        z_half(i).wait_send()
    for d in range(1, NZ):
        z_copy(0, 0, d).wait_send()
    for d in range(1, NZ - 1):
        z_copy(1, 0, d).wait_send()
    for ey in range(NY):
        for ex in range(NX):
            sib_copy(ey, ex, mine_at).wait_send()


PIECES = (2, 2, 2, 4, 1, 1)


def store_kernel(*refs):
    sources, targets, sem = refs[:6], refs[6:12], refs[12]
    copies = []
    for i, (source, target) in enumerate(zip(sources, targets)):
        count = PIECES[i]
        size = source.shape[0] // count
        for j in range(count):
            rows = pl.ds(j * size, size)
            copies.append(pltpu.make_async_copy(source.at[rows], target.at[rows], sem.at[len(copies)]))
    for copy in copies:
        copy.start()
    for copy in copies:
        copy.wait()


def on_device(tokens, cotangent, weight, first_moment, second_moment):
    dma = pltpu.SemaphoreType.DMA
    any_space = pl.BlockSpec(memory_space=pl.ANY)
    rows = lambda *shape: pltpu.VMEM(shape + (D,), F32)
    shapes = [(T, D), (T, D), (T, D), (NY, NZ, NX, 8, D), (4, D), (4, D)]
    held = pl.pallas_call(
        exchange_kernel,
        out_shape=[pltpu.VMEM(shape, F32) for shape in shapes],
        in_specs=[any_space] * 5,
        out_specs=[pl.BlockSpec(memory_space=pltpu.VMEM)] * 6,
        scratch_shapes=[
            rows(T), rows(T), rows(D),
            pltpu.VMEM((D, T), BF16), pltpu.VMEM((D, T), BF16), pltpu.VMEM((D, T), F32),
            pltpu.VMEM((T, D), BF16), pltpu.VMEM((T, D), BF16),
            pltpu.VMEM((T, D), BF16), pltpu.VMEM((T, D), BF16),
            pltpu.VMEM((T, D), BF16), pltpu.VMEM((T, D), BF16),
            rows(NZ, NY, NX, 8), rows(NY - 1, NZ, NX, 8),
            rows(NZ, NX, 8), rows(NZ - 1, NX, 8), rows(2, 2, 2, 8),
            rows(2, NX, 8), rows(2, NX - 1, 8), rows(8), rows(8),
            rows(2, 4), rows(2, 4),
            dma((11,)), dma((2, NY - 1)), dma((2, NY - 1)), dma((2,)), dma((2,)),
            dma((2, NY - 1, NZ)), dma((2, NY - 1, NZ)), dma((2, NZ - 1)), dma((2, NZ - 1)),
            dma((2, NX - 1)), dma((2, NX - 1)), dma((2,)), dma((2,)),
            dma((NZ - 1,)), dma((NZ - 1,)), dma((NX - 1,)), dma((NX - 1,)),
            dma((6,)), dma((6,)), dma((4,)), dma((4,)), dma((2,)), dma((2,)),
            dma((9,)), dma((9,)), dma((3,)), dma((3,)), dma((3 * (NZ - 1),)), dma((3 * (NZ - 1),)),
            dma((6,)), dma((6,)), dma((6,)), dma((6,)),
            dma((NY, NX)), dma((NY, NX)),
        ],
        compiler_params=pltpu.CompilerParams(
            collective_id=0, has_side_effects=True, vmem_limit_bytes=52 * 2**20
        ),
        name="exchange",
    )(tokens, cotangent, weight, first_moment, second_moment)
    projected, input_grad, next_projected, new_weight, new_first, new_second = pl.pallas_call(
        store_kernel,
        out_shape=[jax.ShapeDtypeStruct(shape, F32) for shape in shapes],
        in_specs=[any_space] * 6,
        out_specs=[pl.BlockSpec(memory_space=pltpu.HBM)] * 6,
        scratch_shapes=[dma((sum(PIECES),))],
        compiler_params=pltpu.CompilerParams(vmem_limit_bytes=2**20),
        name="store",
    )(*held)
    new_weight = new_weight.reshape(D, D)
    return (projected, input_grad, new_weight, new_first, new_second, next_projected)


def solution(mesh):
    placed = (P("dp", None), P("dp", None), P(), P("dp", None), P("dp", None))
    return jax.shard_map(
        on_device,
        mesh=mesh,
        in_specs=placed,
        out_specs=(P("dp", None), P("dp", None), P(), P("dp", None), P("dp", None), P("dp", None)),
        check_vma=False,
    )
```

```python
import jax
import jax.numpy as jnp
from jax import lax
from jax.experimental import pallas as pl
from jax.experimental.pallas import tpu as pltpu
from jax.sharding import PartitionSpec as P

beta_one = 0.9
beta_two = 0.999
rate_value = 0.01
step_count = 10
adam_epsilon = 1e-08
norm_epsilon = 1e-06

MESH = pl.DeviceIdType.MESH
NY, NZ, NX = 4, 8, 4
D = 1024
T = 256
CH = D // (NY * NZ)
FAR = (2, 1, 3)
SIDE = 128
F32, BF16 = jnp.float32, jnp.bfloat16


def combine(left_rows, right_rows):
    cross_term = jnp.sum(left_rows * right_rows, axis=-1, keepdims=True)
    left_norm = jnp.sum(left_rows * left_rows, axis=-1, keepdims=True)
    right_norm = jnp.sum(right_rows * right_rows, axis=-1, keepdims=True)
    left_coef = 1.0 - cross_term / (2.0 * (left_norm + norm_epsilon))
    right_coef = 1.0 - cross_term / (2.0 * (right_norm + norm_epsilon))
    return left_coef * left_rows + right_coef * right_rows


def adam_update(gradient, weight_rows, first_rows, second_rows):
    first_new = beta_one * first_rows + (1.0 - beta_one) * gradient
    second_new = beta_two * second_rows + (1.0 - beta_two) * gradient * gradient
    first_hat = first_new / (1.0 - beta_one**step_count)
    second_hat = second_new / (1.0 - beta_two**step_count)
    weight_new = weight_rows - rate_value * first_hat / (jnp.sqrt(second_hat) + adam_epsilon)
    return (weight_new, first_new, second_new)


def split(value):
    high = value.astype(BF16)
    return high, (value - high.astype(F32)).astype(BF16)


def dot(a, b, contract):
    return lax.dot_general(a, b, (contract, ((), ())), preferred_element_type=F32)


def dot3(a_high, a_low, b_high, b_low, contract):
    return (
        dot(a_high, b_high, contract)
        + dot(a_high, b_low, contract)
        + dot(a_low, b_high, contract)
    )


def offset_of(s):
    return 4 + (s + 1) // 2 * (1 - 2 * (s % 2))


def exchange_kernel(
    tok_hbm, cot_hbm, w_hbm, m_hbm, v_hbm,
    proj_v, igrad_v, next_v, wbuf, m_v, v_v,
    tok_v, cot_v, w_v, tth, ttl, ttp, th, tl, thp, tlp, ch, cl,
    g, yr, zs, zr, zz, xs, xr, cs, cr, own_mv, sib_mv,
    in_sem, yhs_sem, yhr_sem, zhs_sem, zhr_sem, ys_sem, yr_sem, zs_sem, zr_sem, xs_sem, xr_sem, cs_sem, cr_sem,
    gzs_sem, gzr_sem, gxs_sem, gxr_sem, gys_sem, gyr_sem, gns_sem, gnr_sem, g2s_sem, g2r_sem,
    y0s_sem, y0r_sem, fis_sem, fir_sem, fzs_sem, fzr_sem, gas_sem, gar_sem, gbs_sem, gbr_sem, gss_sem, gsr_sem,
):
    me = lax.axis_index("dp")
    c = me % 2
    x = me // 2 % NX
    z = me // (2 * NX) % NZ
    y = me // (2 * NX * NZ)
    odd = x % 2 == 1
    even = x % 2 == 0
    owns = [even, odd]
    others = [odd, even]

    def device(yy, zz, xx, cc):
        return (((yy * NZ + zz) * NX + xx) * 2 + cc,)

    def at_y(d):
        return device((y + d) % NY, z, x, c)

    def at_z(d):
        return device(y, (z + d) % NZ, x, c)

    def at_x(d):
        return device(y, z, (x + d) % NX, c)

    sibling = device(y, z, x, 1 - c)

    def far(ex):
        return device((y + 2) % NY, z, (x + ex) % NX, c)

    def remote(src, dst, send, recv, target):
        return pltpu.make_async_remote_copy(
            src_ref=src, dst_ref=dst, send_sem=send, recv_sem=recv,
            device_id=target, device_id_type=MESH,
        )

    quarters = [pl.ds(256 * i, 256) for i in range(4)]
    pairs = [(tok_hbm.at[:, at], tok_v.at[:, at]) for at in quarters]
    pairs += [(cot_hbm.at[:, at], cot_v.at[:, at]) for at in quarters]
    pairs += [(m_hbm, own_mv.at[0]), (v_hbm, own_mv.at[1]), (w_hbm, w_v)]
    loads = [pltpu.make_async_copy(src, dst, in_sem.at[i]) for i, (src, dst) in enumerate(pairs)]
    for load in loads[:10]:
        load.start()

    barrier = pltpu.get_barrier_semaphore()
    partners = (
        [at_y(d) for d in range(1, NY)]
        + [at_z(d) for d in range(1, NZ)]
        + [at_x(d) for d in range(1, NX)]
        + [far(ex) for ex in FAR]
        + [sibling]
    )
    for partner in partners:
        pl.semaphore_signal(barrier, inc=1, device_id=partner, device_id_type=MESH)

    for j in range(D // 128):
        lanes = slice(128 * j, 128 * j + 128)
        if j % 2 == 0:
            loads[j // 2].wait()
        tth[lanes, :], ttl[lanes, :] = split(tok_v[:, lanes].T * (1.0 / T))
    for j in range(D // 256):
        lanes = slice(256 * j, 256 * j + 256)
        loads[4 + j].wait()
        ch[:, lanes], cl[:, lanes] = split(cot_v[:, lanes])
    loads[8].wait()
    loads[9].wait()
    loads[10].start()
    pl.semaphore_wait(barrier, len(partners))

    mv_copy = remote(own_mv, sib_mv, cs_sem.at[1], cr_sem.at[1], sibling)
    mv_copy.start()

    def y_copy(b, s, d):
        rows = pl.ds(2 * b, 2)
        return remote(
            g.at[s, d, rows], yr.at[d - 1, s, rows],
            ys_sem.at[b, d - 1, s], yr_sem.at[b, d - 1, s], at_y(d),
        )

    def y_half(i, d):
        rows = pl.ds(2 + i, 1)
        return remote(
            g.at[NZ - 2, d, rows], yr.at[d - 1, NZ - 2, rows],
            yhs_sem.at[i, d - 1], yhr_sem.at[i, d - 1], at_y(d),
        )

    def z_half(i):
        rows = pl.ds(2 + i, 1)
        return remote(
            zs.at[NZ - 2, rows], zr.at[NZ - 2, rows], zhs_sem.at[i], zhr_sem.at[i], at_z(NZ - 1)
        )

    def z_copy(b, s, d):
        rows = pl.ds(2 * b, 2)
        return remote(
            zs.at[s, rows], zr.at[d - 1, rows], zs_sem.at[b, d - 1], zr_sem.at[b, d - 1], at_z(d)
        )

    def gradient_step(s, carry):
        owner = (z + offset_of(s)) % NZ
        starts = [
            pl.multiple_of((y + d) % NY * (D // NY) + owner * CH, CH) for d in range(NY)
        ]
        high = [tth[pl.ds(start, CH), :] for start in starts]
        low = [ttl[pl.ds(start, CH), :] for start in starts]
        count = NY * CH
        both = dot(jnp.concatenate(high + low, axis=0), ch[...], ((1,), (0,)))
        rest = dot(jnp.concatenate(high, axis=0), cl[...], ((1,), (0,)))
        value = both[:count] + both[count:] + rest
        for d in range(NY):
            for i in range(NX):
                at = d * CH + 8 * i
                g[s, d, 2 * (i % 2) + i // 2] = value[at : at + 8]
        for d in (2, 1, 3):
            y_copy(0, s, d).start()
        return carry

    lax.fori_loop(0, NZ, gradient_step, 0)

    def second_sends(s, carry):
        for d in (2, 1, 3):
            y_copy(1, s, d).start()
        return carry

    lax.fori_loop(0, NZ - 2, second_sends, 0)
    for i in range(2):
        for d in (2, 1, 3):
            y_half(i, d).start()
    second_sends(NZ - 1, 0)

    for j in range(D // 128):
        lanes = slice(128 * j, 128 * j + 128)
        piece = tok_v[:, lanes]
        th[:, lanes], tl[:, lanes] = split(piece)
        turned = piece.T.reshape(4, NX, 8, T)
        plane, quarter = j // 2, j % 2
        for b in range(2):
            at = (2 * b + plane % 2) * 256 + plane // 2 * 128 + quarter * 64
            ttp[at : at + 64] = jnp.stack([turned[:, b], turned[:, b + 2]], axis=1).reshape(64, T)
    loads[10].wait()

    def y_step(b, s):
        for d in range(1, NY):
            y_copy(b, s, d).wait_recv()
        rows = pl.ds(2 * b, 2)
        across = combine(g[s, 0, rows], yr[1, s, rows])
        zs[s, rows] = combine(across, combine(yr[0, s, rows], yr[2, s, rows]))
        z_copy(b, s, offset_of(s)).start()

    def y_step_halves():
        s = NZ - 2
        for i in range(2):
            for d in range(1, NY):
                y_half(i, d).wait_recv()
            q = 2 + i
            across = combine(g[s, 0, q], yr[1, s, q])
            zs[s, q] = combine(across, combine(yr[0, s, q], yr[2, s, q]))
            z_half(i).start()

    def filler(s):
        @pl.when(s < 4)
        def _():
            lanes = pl.ds(pl.multiple_of(s * 256, 256), 256)
            wh, wl = split(w_v[:, lanes])
            proj_v[:, lanes] = dot3(th[...], tl[...], wh, wl, ((1,), (0,)))

        @pl.when(s >= 4)
        def _():
            lanes = pl.ds(pl.multiple_of((s - 4) * 256, 256), 256)
            wh, wl = split(w_v[lanes, :])
            igrad_v[:, lanes] = dot3(ch[...], cl[...], wh, wl, ((1,), (1,)))

    def first_step(s, carry):
        y_step(0, s)
        filler(s)
        return carry

    lax.fori_loop(0, NZ - 1, first_step, 0)

    def z_pair(b, d):
        for at in (d, d + 4):
            z_copy(b, 0, at).wait_recv()
        rows = pl.ds(2 * b, 2)
        return combine(zr[d - 1, rows], zr[d + 3, rows])

    def x_copy(b, d):
        return remote(
            xs.at[b, d], xr.at[b, d - 1], xs_sem.at[b, d - 1], xr_sem.at[b, d - 1], at_x(d)
        )

    def reduce_sends(b):
        zz[b, 0] = z_pair(b, 2)
        zz[b, 1] = z_pair(b, 1)
        for d in (3, 4):
            z_copy(b, 0, d).wait_recv()
        if b == 0:
            z_copy(b, 0, 7).wait_recv()
        last = NZ - 1
        for d in range(1, NY):
            y_copy(b, last, d).wait_recv()

        def early(d):
            h = (x + d) % NX // 2
            q = 2 * b + h
            across = combine(g[last, 0, q], yr[1, last, q])
            across = combine(across, combine(yr[0, last, q], yr[2, last, q]))
            xs[b, d] = combine(combine(across, zr[3, q]), zz[b, 0, h])

        def late(d):
            h = (x + d) % NX // 2
            q = 2 * b + h
            if b == 1:
                z_half(h).wait_recv()
            rest = combine(zz[b, 1, h], combine(zr[2, q], zr[6, q]))
            xs[b, d] = combine(xs[b, d], rest)

        @pl.when(owns[b])
        def _():
            early(2)
            early(0)
            late(2)
            x_copy(b, 2).start()
            late(0)

        @pl.when(others[b])
        def _():
            early(1)
            early(3)
            for d in (1, 3):
                late(d)
                x_copy(b, d).start()

    c_copy = remote(cs, cr, cs_sem.at[0], cr_sem.at[0], sibling)

    def gather_rows(b):
        for d in range(1, NX):
            x_copy(b, d).wait_recv()
        cs[...] = combine(combine(xs[b, 0], xr[b, 1]), combine(xr[b, 0], xr[b, 2]))
        c_copy.start()

    half = D // 2
    mine_at = pl.multiple_of(c * half, half)
    mine_cols = pl.ds(mine_at, half)
    a_cols = pl.ds(mine_at, half // 2)
    b_cols = pl.ds(pl.multiple_of(mine_at + half // 2, half // 2), half // 2)
    a0_cols = pl.ds(mine_at, half - SIDE)
    b0_cols = pl.ds(pl.multiple_of(mine_at + half - SIDE, 128), SIDE)
    far_order = (4, 3, 5, 2, 6, 1, 7)
    order = [3, 1, 2]
    neighbours = [at_x(1), at_x(3), at_y(1), at_y(3)]

    def same(view, send, recv, target):
        return remote(view, view, send, recv, target)

    def z_block(d, target):
        view = wbuf.at[y, (z + d) % NZ, x, :, mine_cols]
        return same(view, gzs_sem.at[target - 1], gzr_sem.at[target - 1], at_z(target))

    def block(ey, ex, cols):
        return wbuf.at[(y + ey) % NY, :, (x + ex) % NX, :, cols]

    def sib_copy(ey, ex, column_start):
        cols = pl.ds(pl.multiple_of(column_start, half), half)
        return same(block(ey, ex, cols), gss_sem.at[ey, ex], gsr_sem.at[ey, ex], sibling)

    def to_sibling(ey, ex):
        sib_copy(ey, ex, mine_at).start()

    def update_rows():
        mv_copy.wait()
        mine, other = own_mv[...], sib_mv[...]
        first = c == 0
        lower, upper = jnp.where(first, mine, other), jnp.where(first, other, mine)
        moments = [jnp.concatenate([lower[i], upper[i]], axis=0) for i in range(2)]
        old_rows = w_v[pl.ds(pl.multiple_of(me // 2 * 8, 8), 8), :]
        c_copy.wait()
        summed = combine(cs[...], cr[...])
        new_rows, new_first, new_second = adam_update(summed, old_rows, moments[0], moments[1])
        wbuf[y, z, x, :, mine_cols] = jnp.where(first, new_rows[:, :half], new_rows[:, half:])
        for d in far_order:
            z_block(0, d).start()
        return first, new_first, new_second

    def keep_moments(first, new_first, new_second):
        m_v[...] = jnp.where(first, new_first[:4], new_first[4:])
        v_v[...] = jnp.where(first, new_second[:4], new_second[4:])

    def x_column(d, ex):
        return same(block(0, ex, mine_cols), gxs_sem.at[d - 1], gxr_sem.at[d - 1], at_x(d))

    def y_column(k, e, ey, ex):
        i = 3 * k + e - 1
        cols = mine_cols if ex % 2 == 0 else a0_cols
        return same(block(ey, ex, cols), gys_sem.at[i], gyr_sem.at[i], at_y(e))

    def y_side(e, d, ex):
        i = 3 * (e - 1) + d - 1
        return same(block(NY - e, ex, b0_cols), y0s_sem.at[i], y0r_sem.at[i], at_x(d))

    def turn(i):
        at = slice(256 * i, 256 * i + 256)
        thp[:, at], tlp[:, at] = split(ttp[at, :].T)

    def following(b, pair, columns):
        for ey in (pair, pair + 2):
            for ex in columns:
                sib_copy(ey, ex, (1 - c) * half).wait_recv()
        p = (y + pair) % 2
        parts = [
            jnp.stack([wbuf[p + 2 * i, :, b], wbuf[p + 2 * i, :, b + 2]], axis=1).reshape(128, D)
            for i in range(2)
        ]
        lanes = pl.ds(pl.multiple_of((2 * b + p) * 256, 256), 256)
        wh, wl = split(jnp.concatenate(parts, axis=0))
        return dot3(thp[:, lanes], tlp[:, lanes], wh, wl, ((1,), (0,)))

    filler(NZ - 1)
    reduce_sends(0)
    for s in range(NZ - 1):
        if s < NZ - 2:
            y_step(1, s)
        else:
            y_step_halves()
        if s in (1, 3, 5, 6):
            turn((1, 3, 5, 6).index(s))
        if s == 1:

            @pl.when(even)
            def _():
                gather_rows(0)

        if s == 2:

            @pl.when(even)
            def _():
                keep_moments(*update_rows())

        if s == 4:

            @pl.when(even)
            def _():
                for d in far_order:
                    z_block(NZ - d, d).wait_recv()
                for d in (2, 1, 3):
                    x_column(d, 0).start()
                to_sibling(0, 0)

    reduce_sends(1)

    def far_block(j, d):
        return wbuf.at[(y + 2) % NY, (z + d) % NZ, (x + NX - FAR[j]) % NX, :, mine_cols]

    def far_first(j):
        return same(far_block(j, 0), fis_sem.at[j], fir_sem.at[j], far(FAR[j]))

    def far_copy(j, at, d):
        i = j * (NZ - 1) + d - 1
        return same(far_block(j, at), fzs_sem.at[i], fzr_sem.at[i], at_z(d))

    def two_away(i, ey, ex):
        target = at_x(2) if i == 0 else at_y(2)
        return same(block(ey, ex, mine_cols), g2s_sem.at[i], g2r_sem.at[i], target)

    def from_neighbour(i):
        ey, ex = [(0, 3), (0, 1), (3, 0), (1, 0)][i]
        return same(block(ey, ex, mine_cols), gns_sem.at[i], gnr_sem.at[i], neighbours[i])

    def a_flow(k, direction, ey):
        i = 2 * k + direction
        return same(block(ey, order[k], a_cols), gas_sem.at[i], gar_sem.at[i], neighbours[2 + direction])

    def b_flow(k, target, ex):
        i = 3 * k + target
        return same(
            block(order[k], ex, b_cols), gbs_sem.at[i], gbr_sem.at[i], at_x((1, 3, 2)[target])
        )

    def y_column_out(k, ex):
        for e in (2, 1, 3):
            y_column(k, e, 0, ex).start()

    def y_column_in(k, ex, d):
        for e in (1, 3, 2):
            y_column(k, e, NY - e, ex).wait_recv()
            if d != 2:
                y_side(e, d, ex).wait_recv()
            to_sibling(NY - e, ex)

    def far_in(js):
        for j in js:
            far_first(j).wait_recv()
            for d in far_order:
                far_copy(j, 0, d).start()

    def far_columns_in(js):
        for j in js:
            for d in far_order:
                far_copy(j, NZ - d, d).wait_recv()
            to_sibling(2, NX - FAR[j])

    def drain(columns, own, js, as_, bs):
        for k, ex in enumerate(columns):
            for e in range(1, NY):
                y_column(k, e, 0, ex).wait_send()
        for d in range(1, NZ):
            z_block(0, d).wait_send()
            for j in js:
                far_copy(j, 0, d).wait_send()
        for k, direction in as_:
            a_flow(k, direction, 0).wait_send()
        for k, target in bs:
            b_flow(k, target, 0).wait_send()

    @pl.when(odd)
    def _():
        def to_neighbours(d):
            view = wbuf.at[y, (z + d) % NZ, x, :, mine_cols]
            for i, target in enumerate(neighbours):
                same(view, gns_sem.at[i], gnr_sem.at[i], target).start()
            same(view, g2s_sem.at[0], g2r_sem.at[0], at_x(2)).start()

        x_column(1, 3).wait_recv()
        x_column(3, 1).wait_recv()
        y_column_out(0, 3)
        y_column_out(1, 1)
        to_sibling(0, 3)
        to_sibling(0, 1)
        gather_rows(1)
        updated = update_rows()
        for i in range(3):
            same(wbuf.at[y, z, x, :, mine_cols], fis_sem.at[i], fir_sem.at[i], far(FAR[i])).start()
        to_neighbours(0)
        keep_moments(*updated)
        for d in (1, 7, 2, 6, 3, 5, 4):
            z_block(NZ - d, d).wait_recv()
            to_neighbours(NZ - d)
        two_away(1, 0, 0).start()
        far_in((0,))
        to_sibling(0, 0)
        for k in range(2):
            from_neighbour(2 + k).wait_recv()
            for target in (0, 1, 2):
                b_flow(k, target, 0).start()
            to_sibling(order[k], 0)
        two_away(0, 0, 2).wait_recv()
        for direction in range(2):
            a_flow(2, direction, 0).start()
        to_sibling(0, 2)
        y_column_in(0, 3, 1)
        y_column_in(1, 1, 3)
        two_away(1, 2, 0).wait_recv()
        to_sibling(2, 0)
        far_columns_in((0,))
        next_v[...] = following(0, 0, (3, 1))
        next_v[...] += following(0, 1, (3, 1))
        next_v[...] += following(1, 0, (0, 2))
        for direction in range(2):
            a_flow(2, direction, order[direction]).wait_recv()
            b_flow(direction, 2, 2).wait_recv()
            to_sibling(order[direction], 2)
        next_v[...] += following(1, 1, (0, 2))
        for i in range(3):
            same(wbuf.at[y, z, x, :, mine_cols], fis_sem.at[i], fir_sem.at[i], far(FAR[i])).wait_send()
        for i in range(4):
            from_neighbour(i).wait_send()
        for i in range(2):
            two_away(i, 0, 0).wait_send()
        for d in (1, 3):
            x_copy(0, d).wait_send()
        x_copy(1, 2).wait_send()
        drain(
            (3, 1), True, (0,), [(2, 0), (2, 1)], [(k, t) for k in range(2) for t in range(3)]
        )

    @pl.when(even)
    def _():
        x_column(2, 2).wait_recv()
        y_column_out(0, 0)
        y_column_out(1, 2)
        to_sibling(0, 2)
        for e in (1, 3, 2):
            y_column(0, e, NY - e, 0).wait_recv()
            for d in (1, 3):
                y_side(e, d, 0).start()
            to_sibling(NY - e, 0)
        far_in((1, 2))
        for k in range(2):
            from_neighbour(k).wait_recv()
            for direction in range(2):
                a_flow(k, direction, 0).start()
            to_sibling(0, order[k])
        y_column_in(1, 2, 2)
        far_columns_in((1, 2))
        next_v[...] = following(0, 0, (0, 2))
        next_v[...] += following(0, 1, (0, 2))
        next_v[...] += following(1, 0, (3, 1))
        for k in range(2):
            for direction in range(2):
                a_flow(k, direction, order[direction]).wait_recv()
                b_flow(direction, k, order[k]).wait_recv()
                to_sibling(order[direction], order[k])
        next_v[...] += following(1, 1, (3, 1))
        for d in range(1, NX):
            x_column(d, 0).wait_send()
            if d != 2:
                for e in range(1, NY):
                    y_side(e, d, 0).wait_send()
        for d in (1, 3):
            x_copy(1, d).wait_send()
        x_copy(0, 2).wait_send()
        drain((0, 2), False, (1, 2), [(k, i) for k in range(2) for i in range(2)], [])

    def y_drain(s, carry):
        for d in range(1, NY):
            y_copy(0, s, d).wait_send()

        @pl.when(s != NZ - 2)
        def _():
            for d in range(1, NY):
                y_copy(1, s, d).wait_send()

        return carry

    lax.fori_loop(0, NZ, y_drain, 0)
    for i in range(2):
        for d in range(1, NY):
            y_half(i, d).wait_send()
        z_half(i).wait_send()
    for d in range(1, NZ):
        z_copy(0, 0, d).wait_send()
    for d in range(1, NZ - 1):
        z_copy(1, 0, d).wait_send()
    for ey in range(NY):
        for ex in range(NX):
            sib_copy(ey, ex, mine_at).wait_send()


PIECES = (2, 2, 2, 4, 1, 1)


def store_kernel(*refs):
    sources, targets, sem = refs[:6], refs[6:12], refs[12]
    copies = []
    for i, (source, target) in enumerate(zip(sources, targets)):
        count = PIECES[i]
        size = source.shape[0] // count
        for j in range(count):
            rows = pl.ds(j * size, size)
            copies.append(pltpu.make_async_copy(source.at[rows], target.at[rows], sem.at[len(copies)]))
    for copy in copies:
        copy.start()
    for copy in copies:
        copy.wait()


def on_device(tokens, cotangent, weight, first_moment, second_moment):
    dma = pltpu.SemaphoreType.DMA
    any_space = pl.BlockSpec(memory_space=pl.ANY)
    rows = lambda *shape: pltpu.VMEM(shape + (D,), F32)
    shapes = [(T, D), (T, D), (T, D), (NY, NZ, NX, 8, D), (4, D), (4, D)]
    held = pl.pallas_call(
        exchange_kernel,
        out_shape=[pltpu.VMEM(shape, F32) for shape in shapes],
        in_specs=[any_space] * 5,
        out_specs=[pl.BlockSpec(memory_space=pltpu.VMEM)] * 6,
        scratch_shapes=[
            rows(T), rows(T), rows(D),
            pltpu.VMEM((D, T), BF16), pltpu.VMEM((D, T), BF16), pltpu.VMEM((D, T), F32),
            pltpu.VMEM((T, D), BF16), pltpu.VMEM((T, D), BF16),
            pltpu.VMEM((T, D), BF16), pltpu.VMEM((T, D), BF16),
            pltpu.VMEM((T, D), BF16), pltpu.VMEM((T, D), BF16),
            rows(NZ, NY, NX, 8), rows(NY - 1, NZ, NX, 8),
            rows(NZ, NX, 8), rows(NZ - 1, NX, 8), rows(2, 2, 2, 8),
            rows(2, NX, 8), rows(2, NX - 1, 8), rows(8), rows(8),
            rows(2, 4), rows(2, 4),
            dma((11,)), dma((2, NY - 1)), dma((2, NY - 1)), dma((2,)), dma((2,)),
            dma((2, NY - 1, NZ)), dma((2, NY - 1, NZ)), dma((2, NZ - 1)), dma((2, NZ - 1)),
            dma((2, NX - 1)), dma((2, NX - 1)), dma((2,)), dma((2,)),
            dma((NZ - 1,)), dma((NZ - 1,)), dma((NX - 1,)), dma((NX - 1,)),
            dma((6,)), dma((6,)), dma((4,)), dma((4,)), dma((2,)), dma((2,)),
            dma((9,)), dma((9,)), dma((3,)), dma((3,)), dma((3 * (NZ - 1),)), dma((3 * (NZ - 1),)),
            dma((6,)), dma((6,)), dma((6,)), dma((6,)),
            dma((NY, NX)), dma((NY, NX)),
        ],
        compiler_params=pltpu.CompilerParams(
            collective_id=0, has_side_effects=True, vmem_limit_bytes=52 * 2**20
        ),
        name="exchange",
    )(tokens, cotangent, weight, first_moment, second_moment)
    projected, input_grad, next_projected, new_weight, new_first, new_second = pl.pallas_call(
        store_kernel,
        out_shape=[jax.ShapeDtypeStruct(shape, F32) for shape in shapes],
        in_specs=[any_space] * 6,
        out_specs=[pl.BlockSpec(memory_space=pltpu.HBM)] * 6,
        scratch_shapes=[dma((sum(PIECES),))],
        compiler_params=pltpu.CompilerParams(vmem_limit_bytes=2**20),
        name="store",
    )(*held)
    new_weight = new_weight.reshape(D, D)
    return (projected, input_grad, new_weight, new_first, new_second, next_projected)


def solution(mesh):
    placed = (P("dp", None), P("dp", None), P(), P("dp", None), P("dp", None))
    return jax.shard_map(
        on_device,
        mesh=mesh,
        in_specs=placed,
        out_specs=(P("dp", None), P("dp", None), P(), P("dp", None), P("dp", None), P("dp", None)),
        check_vma=False,
    )
```
